32 devices in a mesh: phase: 4 (over z), gz: 2 (over y), gy: 4 (over x, core).
Axes of the slice: x: 2, y: 2, z: 4, core: 2. Of those that a mesh axis runs over, the one named last changes fastest.
Arguments:
- volume: bfloat16 [8, 64, 64, 512], P('phase', None, 'gz', 'gy'), may hold values from -6 to 6
- shift_code: int32 [8, 2, 4, 64], P('phase', 'gz', 'gy'), may hold values from 0 to 26, as said below
- frac_code: int32 [8, 2, 4, 64], P('phase', 'gz', 'gy'), may hold values from 0 to 63
- stencil: float32 [4], replicated, may hold values from 0.1 to 0.6
Outputs:
- prior_gradient: float32 [8, 64, 64, 512], P('phase', None, 'gz', 'gy')
The draws below stay inside these ranges and needn't reach their ends.
Inputs may be any that keep to these rules, and one draw needn't show every extreme that they name: `shift_code`: in every phase and region some block has the displacement (1, 1, 1) and another (-1, -1, -1); most displacement components are 0 or 1 in size.
All inputs are finite; a program needn't handle non-finite values.
Results may differ from the reference program's by a relative error of at most 0.00075.
Values may be sent and summed in bfloat16 or wider, within the bound.
A program may use at most 256 MiB of HBM per device.

```python
import jax
import jax.numpy as jnp
from jax import lax

BS = 16
XC = 64
ZC = 32
YC = 128
REACH = 1
PHASES = 8
NZ = 64
NY = 512
BLK = 64
N_GZ = 2
N_GY = 4


def draw_shift_code(key, part):
    uniform_level = jax.random.randint(jax.random.fold_in(key, 505), (PHASES, N_GZ, N_GY, BLK, 3), 0, 16)
    delta = jnp.where(uniform_level < 6, 0, jnp.where(uniform_level < 10, 1, jnp.where(uniform_level < 14, -1, jnp.where(uniform_level == 14, REACH, -REACH))))
    delta = delta.at[:, :, :, 0, :].set(REACH)
    delta = delta.at[:, :, :, 1, :].set(-REACH)
    side = 2 * REACH + 1
    code = ((delta[..., 0] + REACH) * side + delta[..., 1] + REACH) * side + delta[..., 2] + REACH
    return code.astype(jnp.int32)


def set_ends(array, own_key, low, high):
    place = [jax.random.randint(jax.random.fold_in(own_key, axis), (), 0, length) for axis, length in enumerate(array.shape)]
    main_axis = array.shape.index(max(array.shape))
    neighbour = place[:main_axis] + [(place[main_axis] + 1) % array.shape[main_axis]] + place[main_axis + 1:]
    return array.at[tuple(place)].set(low).at[tuple(neighbour)].set(high)


def steps_of(stream_key, shape, pieces, least, high):
    factor_of = 1.0
    for dim, parts in pieces:
        draws = jax.random.uniform(jax.random.fold_in(jax.random.fold_in(stream_key, 6), dim), (parts,), jnp.float32, least / len(pieces), high / len(pieces))
        factor_of = factor_of * jnp.repeat(jnp.exp(draws), shape[dim] // parts).reshape((-1,) + (1,) * (len(shape) - 1 - dim))
    return factor_of


def bell_draw(key, extent, deviation, reach, shards=(), held_as=jnp.bfloat16):
    values = deviation * jax.random.normal(key, extent, jnp.float32)
    if shards:
        values = values * steps_of(key, extent, shards, -0.22, 0.18)
    return jnp.clip(values, -reach, reach).astype(held_as)


def setup_inputs(seed: int = 0) -> dict:
    key_list = jax.random.split(jax.random.key(seed), 5)
    volume = bell_draw(key_list[0], (PHASES, XC, NZ, NY), 1.0, 6.0, ((0, 4), (2, 2), (3, 4)))
    shift_code = draw_shift_code(jax.random.fold_in(key_list[4], 71), 0)
    frac_code = set_ends(jax.random.randint(key_list[2], (PHASES, N_GZ, N_GY, BLK), 0, 64), jax.random.fold_in(key_list[2], 1), 0, 63).astype(jnp.int32)
    stencil = jnp.clip(jax.random.uniform(key_list[3], (4,), jnp.float32, 0.1, 0.6), 0.1, 0.6)
    return {"volume": volume, "shift_code": shift_code, "frac_code": frac_code, "stencil": stencil}


def fraction_table():
    code_range = jnp.arange(64)
    levels = jnp.stack([code_range // 16 + 1, code_range // 4 % 4 + 1, code_range % 4 + 1], axis=1)
    return levels.astype(jnp.float32) / 5.0


def block_matrices(code_list, block_edge):
    onehot = (code_list[:, None] == jnp.arange(64)[None, :]).astype(jnp.float32)
    fractions = jnp.dot(onehot, fraction_table(), precision=lax.Precision.HIGHEST)
    position = jnp.arange(block_edge)
    identity = (position[:, None] == position[None, :]).astype(jnp.float32)
    forward_shift = (jnp.minimum(position + 1, block_edge - 1)[:, None] == position[None, :]).astype(jnp.float32)
    return (1.0 - fractions)[:, :, None, None] * identity + fractions[:, :, None, None] * forward_shift


def warp_blocks(source, matrices):
    along_first = jnp.einsum("nai,nijk->najk", matrices[:, 0], source, precision=lax.Precision.HIGHEST)
    second = jnp.einsum("nbj,najk->nabk", matrices[:, 1], along_first, precision=lax.Precision.HIGHEST)
    return jnp.einsum("nck,nabk->nabc", matrices[:, 2], second, precision=lax.Precision.HIGHEST)


def adjoint_blocks(source, matrices):
    along_first = jnp.einsum("nia,nijk->najk", matrices[:, 0], source, precision=lax.Precision.HIGHEST)
    second = jnp.einsum("njb,najk->nabk", matrices[:, 1], along_first, precision=lax.Precision.HIGHEST)
    return jnp.einsum("nkc,nabk->nabc", matrices[:, 2], second, precision=lax.Precision.HIGHEST)


def smooth(padded, stencil):
    center = padded[..., 1:-1, 1:-1, 1:-1]
    along_x = padded[..., 2:, 1:-1, 1:-1] + padded[..., :-2, 1:-1, 1:-1]
    along_z = padded[..., 1:-1, 2:, 1:-1] + padded[..., 1:-1, :-2, 1:-1]
    along_y = padded[..., 1:-1, 1:-1, 2:] + padded[..., 1:-1, 1:-1, :-2]
    return stencil[0] * center + stencil[1] * along_x + stencil[2] * along_z + stencil[3] * along_y


def volume_blocks(phase_volume):
    shaped = phase_volume.reshape(XC // BS, BS, N_GZ, ZC // BS, BS, N_GY, YC // BS, BS)
    return shaped.transpose(2, 5, 0, 3, 6, 1, 4, 7).reshape(-1, BS, BS, BS)


def block_volume(blocks):
    shaped = blocks.reshape(N_GZ, N_GY, XC // BS, ZC // BS, YC // BS, BS, BS, BS)
    return shaped.transpose(2, 5, 0, 3, 6, 1, 4, 7).reshape(XC, NZ, NY)


def source_index(codes):
    x_blocks = XC // BS
    z_blocks = ZC // BS
    y_blocks = YC // BS
    side = 2 * REACH + 1
    codes = codes.reshape(N_GZ, N_GY, BLK).astype(jnp.int32)
    local = jnp.arange(BLK).astype(jnp.int32)
    block_x = local // (z_blocks * y_blocks)
    block_z = local // y_blocks % z_blocks
    block_y = local % y_blocks
    region_z = jnp.arange(N_GZ).astype(jnp.int32)[:, None, None]
    region_y = jnp.arange(N_GY).astype(jnp.int32)[None, :, None]
    delta_x = codes // (side * side) - REACH
    delta_z = codes // side % side - REACH
    delta_y = codes % side - REACH
    source_x = jnp.clip(block_x + delta_x, 0, x_blocks - 1)
    source_z = jnp.clip(region_z * z_blocks + block_z + delta_z, 0, N_GZ * z_blocks - 1)
    source_y = jnp.clip(region_y * y_blocks + block_y + delta_y, 0, N_GY * y_blocks - 1)
    region = (source_z // z_blocks) * N_GY + source_y // y_blocks
    inside = (source_x * z_blocks + source_z % z_blocks) * y_blocks + source_y % y_blocks
    return (region * BLK + inside).reshape(-1).astype(jnp.int32)


def reference(volume, shift_code, frac_code, stencil):
    groups = N_GZ * N_GY
    upcoming = jnp.roll(volume, -1, axis=0)

    def forward(items):
        phase_volume, next_phase, codes, code_list = items
        blocks = volume_blocks(phase_volume)
        targets = source_index(codes)
        source = blocks[targets].astype(jnp.float32)
        matrices = block_matrices(code_list.reshape(-1), BS)
        residual = warp_blocks(source, matrices) - volume_blocks(next_phase).astype(jnp.float32)
        residual = block_volume(residual)
        return smooth(jnp.pad(residual, 1), stencil)

    smoothed = lax.map(forward, (volume, upcoming, shift_code, frac_code))

    def backward(items):
        phase_smooth, codes, code_list = items
        targets = source_index(codes)
        matrices = block_matrices(code_list.reshape(-1), BS)
        pulled = adjoint_blocks(volume_blocks(phase_smooth), matrices).reshape(groups * BLK, BS * BS * BS)
        summed = jax.ops.segment_sum(pulled, targets, num_segments=groups * BLK)
        return block_volume(summed.reshape(-1, BS, BS, BS))

    adjoint = lax.map(backward, (smoothed, shift_code, frac_code))
    return adjoint - jnp.roll(smoothed, 1, axis=0)
```

```python
import functools

import jax
import jax.numpy as jnp
from jax import lax
from jax.experimental import pallas as pl
from jax.experimental.pallas import tpu as pltpu
from jax.sharding import PartitionSpec as P

BS = 16
DIRS = ((-1, 0), (1, 0), (0, -1), (0, 1), (-1, -1), (-1, 1), (1, -1), (1, 1))
MESH = pl.DeviceIdType.MESH
F32 = jnp.float32
BF16 = jnp.bfloat16


def roll(x, shift, axis):
    size = x.shape[axis]
    shift = shift % size
    return x if shift == 0 else pltpu.roll(x, shift, axis)


def kernel(
    sizes, vol_in, shift, frac, stencil, out,
    vol, nxt, zh, yh, ch, pk, wide, codes, offs, places, fracs, gath, resid, fz, fy, rz, ry,
    smo, pulled, own, az, azr, oy, oyr, ocr, ssem, rsem, lsem,
):
    n_phase, n_gz, n_gy = sizes
    phases, cells_x, cells_z, cells_y = vol.shape
    xb_n, zb_n, yb_n = cells_x // BS, cells_z // BS, cells_y // BS
    per = yb_n // xb_n
    quads = BS // per
    rows = xb_n * zb_n
    me_p, me_z, me_y = lax.axis_index("phase"), lax.axis_index("gz"), lax.axis_index("gy")

    def exists(dz, dy):
        z, y = me_z + dz, me_y + dy
        return (z >= 0) & (z < n_gz) & (y >= 0) & (y < n_gy)

    def target(dz, dy):
        return {
            "gz": jnp.clip(me_z + dz, 0, n_gz - 1),
            "gy": jnp.clip(me_y + dy, 0, n_gy - 1),
        }

    following = {"phase": lax.rem(me_p + 1, n_phase)}
    previous = {"phase": lax.rem(me_p + n_phase - 1, n_phase)}

    def remote(src, dst, idx, where):
        return pltpu.make_async_remote_copy(
            src_ref=src, dst_ref=dst, send_sem=ssem.at[idx], recv_sem=rsem.at[idx],
            device_id=where, device_id_type=MESH,
        )

    def halo(t, d):
        dz, dy = DIRS[d]
        rows_z = slice(0, BS) if dz < 0 else slice(cells_z - BS, cells_z)
        if dy == 0:
            src, dst = vol.at[t, :, rows_z, :], zh.at[d, t]
        elif dz == 0:
            src, dst = pk.at[d - 2, t], yh.at[d - 2, t]
        else:
            src, dst = pk.at[0 if dy < 0 else 1, t, :, rows_z, :], ch.at[d - 4, t]
        return remote(src, dst, t * 8 + d, target(dz, dy))

    def ring(s, d):
        dz, dy = DIRS[d]
        src, dst = (fz.at[d, s], rz.at[d, s]) if dy == 0 else (fy.at[s], ry.at[d - 2, s])
        return remote(src, dst, 8 * phases + s * 4 + d, target(dz, dy))

    base_adj = 8 * phases + 4 * (phases + 1)

    def adj(t, d):
        dz, dy = DIRS[d]
        row = 0 if dz < 0 else (zb_n + 1 if dz > 0 else None)
        if dy == 0:
            src, dst = az.at[d, t], azr.at[d, t]
        elif dz == 0:
            src, dst = oy.at[d - 2, t, :, BS:BS + cells_z, :], oyr.at[d - 2, t]
        else:
            src = oy.at[0 if dy < 0 else 1, t, :, row * BS:(row + 1) * BS, :]
            dst = ocr.at[d - 4, t]
        return remote(src, dst, base_adj + t * 8 + d, target(dz, dy))

    base_p = base_adj + 8 * phases
    follow_copy = remote(vol.at[0], nxt, base_p, previous)
    frac_copy = remote(fracs.at[phases], fracs.at[0], base_p + 1, following)
    source_copies = [
        remote(gath.at[phases, xb * BS:(xb + 1) * BS], gath.at[0, xb * BS:(xb + 1) * BS], base_p + 2 + xb, following)
        for xb in range(xb_n)
    ]

    def start(make, ds):
        for d in ds:
            pl.when(exists(*DIRS[d]))(lambda d=d: make(d).start())

    def arrive(make, ds):
        for d in ds:
            dz, dy = DIRS[d]
            pl.when(exists(-dz, -dy))(lambda d=d: make(d).wait_recv())

    def sent(make, ds):
        for d in ds:
            pl.when(exists(*DIRS[d]))(lambda d=d: make(d).wait_send())

    fetch = pltpu.make_async_copy(vol_in, vol, lsem.at[0])
    fetch.start()
    barrier = pltpu.get_barrier_semaphore()
    count = 2
    for d in range(8):
        here = exists(*DIRS[d])
        count = count + here.astype(jnp.int32)

        @pl.when(here)
        def _(d=d):
            pl.semaphore_signal(barrier, inc=1, device_id=target(*DIRS[d]), device_id_type=MESH)

    for where in (following, previous):
        pl.semaphore_signal(barrier, inc=1, device_id=where, device_id_type=MESH)
    lane = lax.broadcasted_iota(jnp.int32, (BS, cells_y), 1)
    sub = lax.broadcasted_iota(jnp.int32, (BS, cells_y), 0)
    lane_blk = lane // BS
    lane_half = lane_blk.astype(F32).astype(BF16)
    row_of = lax.broadcasted_iota(jnp.int32, (rows, cells_y), 0)
    row_blk = lax.broadcasted_iota(jnp.int32, (rows, cells_y), 1) // BS
    lane_in = lane - lane_blk * BS
    lane_z = lax.broadcasted_iota(jnp.int32, (cells_z, cells_y), 1)
    blk_z = lane_z // BS

    fetch.wait()
    for t in range(phases):
        def pack(q, carry, t=t):
            lo = jnp.zeros((cells_z, cells_y), F32)
            hi = jnp.zeros((cells_z, cells_y), F32)
            for xb in range(xb_n):
                for j in range(per):
                    k = xb * per + j
                    plane = vol[t, xb * BS + q * per + j].astype(F32)
                    lo = jnp.where(blk_z == k, roll(plane, BS * k, 1), lo)
                    hi = jnp.where(blk_z == k, roll(plane, BS * k + BS, 1), hi)
            pk[0, t, q] = lo.astype(BF16)
            pk[1, t, q] = hi.astype(BF16)
            return carry

        lax.fori_loop(0, quads, pack, 0)

    pl.semaphore_wait(barrier, count)
    follow_copy.start()
    for t in range(phases):
        start(functools.partial(halo, t), (4, 5, 6, 7, 0, 1, 2, 3))

    for t in range(phases):
        c = jnp.zeros((rows, cells_y), jnp.int32)
        f = jnp.zeros((rows, cells_y), jnp.int32)
        for row in range(rows):
            cr = jnp.zeros((1, cells_y), jnp.int32)
            fr = jnp.zeros((1, cells_y), jnp.int32)
            for k in range(yb_n):
                cr = jnp.where(lane_blk[:1] == k, shift[t, row * yb_n + k], cr)
                fr = jnp.where(lane_blk[:1] == k, frac[t, row * yb_n + k], fr)
            c = jnp.where(row_of == row, cr, c)
            f = jnp.where(row_of == row, fr, f)
        one = lambda m: m.astype(jnp.int32)
        dx = one(c >= 9) + one(c >= 18)
        c = c - 9 * dx
        dz = one(c >= 3) + one(c >= 6)
        dy = c - 3 * dz
        bx, bz = row_of // zb_n, row_of % zb_n
        ex = jnp.clip(bx + dx - 1, 0, xb_n - 1) - bx + 1
        gz0 = me_z * zb_n + bz
        ez = jnp.clip(gz0 + dz - 1, 0, n_gz * zb_n - 1) - gz0 + 1
        gy0 = me_y * yb_n + row_blk
        ey = jnp.clip(gy0 + dy - 1, 0, n_gy * yb_n - 1) - gy0 + 1
        codes[t] = ex * 9 + ez * 3 + ey
        offs[t] = (ey * (zb_n + 2) + bz + ez) * cells_x + (bx + ex - 1) * BS
        for i, level in enumerate((f // 16, (f // 4) % 4, f % 4)):
            fracs[t + 1, i] = jnp.where(
                level == 0, F32(1 / 5), jnp.where(
                    level == 1, F32(2 / 5), jnp.where(level == 2, F32(3 / 5), F32(4 / 5))))
    frac_copy.start()
    place = pltpu.make_async_copy(offs, places, lsem.at[1])
    place.start()

    for d in range(8):
        dz, dy = DIRS[d]

        @pl.when(jnp.logical_not(exists(-dz, -dy)))
        def _(d=d, dz=dz, dy=dy):
            if dy == 0:
                rz[d] = jnp.zeros(rz.shape[1:], F32)
                azr[d] = jnp.zeros(azr.shape[1:], BF16)
            elif dz == 0:
                ry[d - 2] = jnp.zeros(ry.shape[1:], F32)
                oyr[d - 2] = jnp.zeros(oyr.shape[1:], BF16)
            else:
                ocr[d - 4] = jnp.zeros(ocr.shape[1:], BF16)
    for s in range(phases + 1):
        resid[s, 0] = jnp.zeros((cells_z, cells_y), F32)
        resid[s, cells_x + 1] = jnp.zeros((cells_z, cells_y), F32)

    def widen(t, parts):
        def body(q, carry):
            for ze in parts:
                if ze == 0:
                    left, right = ch[7 - 4, t, q], ch[6 - 4, t, q]
                elif ze == zb_n + 1:
                    left, right = ch[5 - 4, t, q], ch[4 - 4, t, q]
                else:
                    at = slice((ze - 1) * BS, ze * BS)
                    left, right = yh[1, t, q, at, :], yh[0, t, q, at, :]
                left, right = left.astype(F32), right.astype(F32)
                for xb in range(xb_n):
                    for j in range(per):
                        k = xb * per + j
                        x = xb * BS + q * per + j
                        if ze == 0:
                            plane = zh[1, t, x]
                        elif ze == zb_n + 1:
                            plane = zh[0, t, x]
                        else:
                            plane = vol[t, x, (ze - 1) * BS:ze * BS, :]
                        wide[t, (zb_n + 2 + ze) * cells_x + x] = plane
                        plane = plane.astype(F32)
                        wide[t, ze * cells_x + x] = jnp.where(
                            lane < BS, roll(left, -BS * k, 1), roll(plane, BS, 1)).astype(BF16)
                        wide[t, (2 * zb_n + 4 + ze) * cells_x + x] = jnp.where(
                            lane >= cells_y - BS, roll(right, -BS - BS * k, 1), roll(plane, -BS, 1)).astype(BF16)
            return carry

        lax.fori_loop(0, quads, body, 0)

    def gather(t, lo, hi):
        def body(row, carry):
            xb, zb = row // zb_n, row % zb_n
            acc = None
            for k in range(yb_n):
                cand = wide[t, pl.ds(places[t, row, k * BS], BS)]
                acc = cand if acc is None else jnp.where((lane_half == k)[None], cand, acc)
            xs = pl.ds(pl.multiple_of(xb * BS, BS), BS)
            zs = pl.ds(pl.multiple_of(zb * BS, BS), BS)
            gath[t + 1, xs, zs, :] = acc
            return carry

        lax.fori_loop(lo * zb_n, hi * zb_n, body, 0)

    def factors(s, row):
        fx, fz_, fy_ = (
            jnp.broadcast_to(fracs[s, i, pl.ds(row, 1), :], (BS, cells_y)) for i in range(3))
        return fx, jnp.where(sub == BS - 1, 0.0, fz_), jnp.where(lane_in == BS - 1, 0.0, fy_)

    def warp(s, lo_x, hi_x):
        upcoming = vol.at[s] if s < phases else nxt

        def body(row, carry):
            xb, zb = row // zb_n, row % zb_n
            xs = pl.ds(pl.multiple_of(xb * BS, BS), BS)
            zs = pl.ds(pl.multiple_of(zb * BS, BS), BS)
            fx, fz_, fy_ = factors(s, row)
            v = gath[s, xs, zs, :].astype(F32)
            face = jnp.zeros((BS, cells_y), F32)
            for a in range(BS):
                p = v[a]
                if a < BS - 1:
                    p = p + fx * (v[a + 1] - p)
                p = p + fz_ * (roll(p, -1, 0) - p)
                p = p + fy_ * (roll(p, -1, 1) - p)
                p = p - upcoming[xb * BS + a, zs, :].astype(F32)
                resid[s, 1 + xb * BS + a, zs, :] = p
                face = jnp.where(lane // 2 == a, roll(p, 2 * a + 1, 1), face)
            fy[s, xb, zs, :] = face

            def z_face(side, z):
                fz[side, s, xs, :] = jnp.concatenate(
                    [resid[s, 1 + xb * BS + a, z:z + 1, :] for a in range(BS)], axis=0)

            pl.when((zb == 0) & exists(-1, 0))(lambda: z_face(0, 0))
            pl.when((zb == zb_n - 1) & exists(1, 0))(lambda: z_face(1, cells_z - 1))

            return carry

        lax.fori_loop(lo_x * zb_n, hi_x * zb_n, body, 0)
        if hi_x == xb_n:
            start(functools.partial(ring, s), range(4))

    sub_z = lax.broadcasted_iota(jnp.int32, (cells_z, cells_y), 0)

    def smooth(s):
        arrive(functools.partial(ring, s), range(4))
        w0, w1, w2, w3 = stencil[0], stencil[1], stencil[2], stencil[3]

        def body(xb, carry):
            sides = jnp.where(lane_z % 2 == 1, roll(ry[1, s, xb], 1, 1), roll(ry[0, s, xb], -1, 1))
            below = rz[1, s, pl.ds(pl.multiple_of(xb * BS, BS), BS), :]
            above = rz[0, s, pl.ds(pl.multiple_of(xb * BS, BS), BS), :]
            for a in range(BS):
                x = xb * BS + a
                c = resid[s, x + 1]
                along_x = resid[s, x] + resid[s, x + 2]
                up = jnp.where(sub_z == 0, jnp.broadcast_to(below[a:a + 1], c.shape), roll(c, 1, 0))
                dn = jnp.where(sub_z == cells_z - 1, jnp.broadcast_to(above[a:a + 1], c.shape), roll(c, -1, 0))
                ends = roll(sides, -2 * a - 1, 1)
                yl = jnp.where(lane_z == 0, ends, roll(c, 1, 1))
                yr = jnp.where(lane_z == cells_y - 1, ends, roll(c, -1, 1))
                total = w0 * c + w1 * along_x + w2 * (up + dn) + w3 * (yl + yr)
                if s == 0:
                    out[0, x] = out[0, x] - total
                else:
                    smo[s, x] = total
            return carry

        lax.fori_loop(0, xb_n, body, 0)

    def pull(t):
        def body(row, carry):
            xb, zb = row // zb_n, row % zb_n
            zs = pl.ds(pl.multiple_of(zb * BS, BS), BS)
            fx, fz_, fy_ = factors(t + 1, row)
            last = None
            for a in range(BS):
                p = smo[t + 1, xb * BS + a, zs, :]
                g = fz_ * p
                p = p - g + roll(g, 1, 0)
                g = fy_ * p
                p = p - g + roll(g, 1, 1)
                g = fx * p
                r = p if a == BS - 1 else p - g
                if last is not None:
                    r = r + last
                last = g
                pulled[t, xb * BS + a, zs, :] = r
            return carry

        lax.fori_loop(0, rows, body, 0)

    def scatter(t, parts):
        def body(q, carry):
            for ze in parts:
                pack_lo = jnp.zeros((BS, cells_y), F32)
                pack_hi = jnp.zeros((BS, cells_y), F32)
                for xs in range(xb_n):
                    accs = [jnp.zeros((per, BS, cells_y), F32) for _ in range(3)]
                    for dx in (-1, 0, 1):
                        for dz in (-1, 0, 1):
                            xd, zd = xs - dx, ze - 1 - dz
                            if not (0 <= xd < xb_n and 0 <= zd < zb_n):
                                continue
                            code = codes[t, pl.ds(xd * zb_n + zd, 1), :]
                            p = pulled[t, pl.ds(xd * BS + q * per, per), zd * BS:(zd + 1) * BS, :]
                            for dy in (-1, 0, 1):
                                hit = code == (dx + 1) * 9 + (dz + 1) * 3 + dy + 1
                                accs[dy + 1] = accs[dy + 1] + jnp.where(hit[None], p, 0.0)
                    for j in range(per):
                        k = xs * per + j
                        x = xs * BS + q * per + j
                        minus, zero, plus = accs[0][j], accs[1][j], accs[2][j]
                        total = (
                            zero
                            + jnp.where(lane >= BS, roll(plus, BS, 1), 0.0)
                            + jnp.where(lane < cells_y - BS, roll(minus, -BS, 1), 0.0)
                        )
                        pack_hi = jnp.where(lane_blk == k, roll(plus, BS + BS * k, 1), pack_hi)
                        pack_lo = jnp.where(lane_blk == k, roll(minus, BS * k, 1), pack_lo)
                        if ze == 0:
                            az[0, t, x] = total.astype(BF16)
                        elif ze == zb_n + 1:
                            az[1, t, x] = total.astype(BF16)
                        else:
                            own[t, x, (ze - 1) * BS:ze * BS, :] = total
                oy[0, t, q, ze * BS:(ze + 1) * BS, :] = pack_lo.astype(BF16)
                oy[1, t, q, ze * BS:(ze + 1) * BS, :] = pack_hi.astype(BF16)
            return carry

        lax.fori_loop(0, quads, body, 0)

    def finish(t):
        def body(q, carry):
            for zb in range(zb_n):
                at = slice(zb * BS, (zb + 1) * BS)
                left, right = oyr[1, t, q, at, :].astype(F32), oyr[0, t, q, at, :].astype(F32)
                if zb == 0:
                    left = left + ocr[7 - 4, t, q].astype(F32)
                    right = right + ocr[6 - 4, t, q].astype(F32)
                if zb == zb_n - 1:
                    left = left + ocr[5 - 4, t, q].astype(F32)
                    right = right + ocr[4 - 4, t, q].astype(F32)
                for xb in range(xb_n):
                    for j in range(per):
                        k = xb * per + j
                        x = xb * BS + q * per + j
                        p = own[t, x, at, :]
                        if zb == 0:
                            p = p + azr[1, t, x].astype(F32)
                        if zb == zb_n - 1:
                            p = p + azr[0, t, x].astype(F32)
                        p = p + jnp.where(lane < BS, roll(left, -BS * k, 1), 0.0)
                        p = p + jnp.where(lane >= cells_y - BS, roll(right, -BS - BS * k, 1), 0.0)
                        out[t, x, at, :] = p if t == 0 else p - smo[t, x, at, :]
            return carry

        lax.fori_loop(0, quads, body, 0)

    inner = range(1, zb_n + 1)

    def at_edges(work, t):
        pl.when(exists(-1, 0))(lambda: work(t, (0,)))
        pl.when(exists(1, 0))(lambda: work(t, (zb_n + 1,)))

    for t in range(phases):
        arrive(functools.partial(halo, t), (2, 3))
        widen(t, inner)
    place.wait()
    for t in range(phases):
        arrive(functools.partial(halo, t), (0, 1, 4, 5, 6, 7))
        at_edges(widen, t)
        if t == phases - 1:
            for xb in range(xb_n):
                gather(t, xb, xb + 1)
                source_copies[xb].start()
            follow_copy.wait_recv()
        else:
            gather(t, 0, xb_n)
        warp(t + 1, 0, xb_n)
        smooth(t + 1)
        pull(t)
        at_edges(scatter, t)
        start(functools.partial(adj, t), (0, 1, 4, 5, 6, 7))
        scatter(t, inner)
        start(functools.partial(adj, t), (2, 3))
    arrive(functools.partial(adj, 0), range(8))
    finish(0)
    frac_copy.wait_recv()
    for xb in range(xb_n):
        source_copies[xb].wait_recv()
        warp(0, xb, xb + 1)
    for t in range(1, phases):
        arrive(functools.partial(adj, t), range(8))
        finish(t)
    smooth(0)
    for t in range(phases):
        sent(functools.partial(halo, t), range(8))
        sent(functools.partial(adj, t), range(8))
    for s in range(phases + 1):
        sent(functools.partial(ring, s), range(4))
    for copy in (follow_copy, frac_copy, *source_copies):
        copy.wait_send()


def body(sizes, volume, shift_code, frac_code, stencil):
    t, x, z, y = volume.shape
    xb, zb, yb = x // BS, z // BS, y // BS
    quads = BS * xb // yb
    rows = xb * zb
    blocks = shift_code.shape[-1]
    n_sem = 16 * t + 4 * (t + 1) + 2 + xb
    V = pltpu.VMEM
    scratch = [
        V((t, x, z, y), BF16),
        V((x, z, y), BF16),
        V((2, t, x, BS, y), BF16),
        V((2, t, quads, z, y), BF16),
        V((4, t, quads, BS, y), BF16),
        V((2, t, quads, z, y), BF16),
        V((t, 3 * (zb + 2) * x, BS, y), BF16),
        V((t, rows, y), jnp.int32),
        V((t, rows, y), jnp.int32),
        pltpu.SMEM((t, rows, y), jnp.int32),
        V((t + 1, 3, rows, y), F32),
        V((t + 1, x, z, y), BF16),
        V((t + 1, x + 2, z, y), F32),
        V((2, t + 1, x, y), F32),
        V((t + 1, xb, z, y), F32),
        V((2, t + 1, x, y), F32),
        V((2, t + 1, xb, z, y), F32),
        V((t + 1, x, z, y), F32),
        V((t, x, z, y), F32),
        V((t, x, z, y), F32),
        V((2, t, x, BS, y), BF16),
        V((2, t, x, BS, y), BF16),
        V((2, t, quads, z + 2 * BS, y), BF16),
        V((2, t, quads, z, y), BF16),
        V((4, t, quads, BS, y), BF16),
        pltpu.SemaphoreType.DMA((n_sem,)),
        pltpu.SemaphoreType.DMA((n_sem,)),
        pltpu.SemaphoreType.DMA((2,)),
    ]
    vm, sm = pl.BlockSpec(memory_space=pltpu.VMEM), pl.BlockSpec(memory_space=pltpu.SMEM)
    return pl.pallas_call(
        functools.partial(kernel, sizes),
        out_shape=pltpu.VMEM((t, x, z, y), F32),
        in_specs=[pl.BlockSpec(memory_space=pl.ANY), sm, sm, sm],
        out_specs=vm,
        scratch_shapes=scratch,
        compiler_params=pltpu.CompilerParams(
            collective_id=0, has_side_effects=True, vmem_limit_bytes=60 * 1024 * 1024
        ),
    )(volume, shift_code.reshape(t, blocks), frac_code.reshape(t, blocks), stencil)


def solution(mesh):
    placed = (
        P("phase", None, "gz", "gy"),
        P("phase", "gz", "gy", None),
        P("phase", "gz", "gy", None),
        P(),
    )
    sizes = tuple(mesh.shape[name] for name in ("phase", "gz", "gy"))
    return jax.shard_map(
        functools.partial(body, sizes), mesh=mesh, in_specs=placed,
        out_specs=P("phase", None, "gz", "gy"), check_vma=False,
    )
```

```python
import functools

import jax
import jax.numpy as jnp
from jax import lax
from jax.experimental import pallas as pl
from jax.experimental.pallas import tpu as pltpu
from jax.sharding import PartitionSpec as P

BS = 16
EARLY_HALO = 2
EARLY_ADJ = 3
DIRS = ((-1, 0), (1, 0), (0, -1), (0, 1), (-1, -1), (-1, 1), (1, -1), (1, 1))
MESH = pl.DeviceIdType.MESH
F32 = jnp.float32
BF16 = jnp.bfloat16


def roll(x, shift, axis):
    size = x.shape[axis]
    shift = shift % size
    return x if shift == 0 else pltpu.roll(x, shift, axis)


def kernel(
    sizes, vol_in, shift, frac, stencil, out,
    vol, nxt, zh, yh, ch, pk, wide, codes, offs, places, fracs, gath, resid, fz, fy, rz, ry,
    smo, pulled, own, az, azr, oy, oyr, ocr, ssem, rsem, lsem,
):
    n_phase, n_gz, n_gy = sizes
    phases, cells_x, cells_z, cells_y = vol.shape
    xb_n, zb_n, yb_n = cells_x // BS, cells_z // BS, cells_y // BS
    per = yb_n // xb_n
    quads = BS // per
    rows = xb_n * zb_n
    me_p, me_z, me_y = lax.axis_index("phase"), lax.axis_index("gz"), lax.axis_index("gy")

    def exists(dz, dy):
        z, y = me_z + dz, me_y + dy
        return (z >= 0) & (z < n_gz) & (y >= 0) & (y < n_gy)

    def target(dz, dy):
        return {
            "gz": jnp.clip(me_z + dz, 0, n_gz - 1),
            "gy": jnp.clip(me_y + dy, 0, n_gy - 1),
        }

    following = {"phase": lax.rem(me_p + 1, n_phase)}
    previous = {"phase": lax.rem(me_p + n_phase - 1, n_phase)}

    def remote(src, dst, idx, where):
        return pltpu.make_async_remote_copy(
            src_ref=src, dst_ref=dst, send_sem=ssem.at[idx], recv_sem=rsem.at[idx],
            device_id=where, device_id_type=MESH,
        )

    parts = xb_n
    one_z = 2 * parts
    base_y = phases * one_z
    base_ring = base_y + 6 * phases
    base_az = base_ring + 4 * (phases + 1)
    base_ay = base_az + phases * one_z
    base_p = base_ay + 6 * phases

    def halo_z(t, p, d):
        dz, dy = DIRS[d]
        rows_z = slice(0, BS) if dz < 0 else slice(cells_z - BS, cells_z)
        at = slice(p * BS, (p + 1) * BS)
        return remote(
            vol_in.at[t, at, rows_z, :], zh.at[d, t, at], t * one_z + d * parts + p, target(dz, dy))

    def halo(t, d):
        return remote(pk.at[d - 2, t], yh.at[d - 2, t], base_y + t * 6 + d - 2, target(*DIRS[d]))

    def corner(t, d):
        dz, dy = DIRS[d]
        rows_z = slice(0, BS) if dz < 0 else slice(cells_z - BS, cells_z)
        return remote(
            pk.at[0 if dy < 0 else 1, t, :, rows_z, :], ch.at[d - 4, t],
            base_y + t * 6 + d - 2, target(dz, dy))

    def ring(s, d):
        dz, dy = DIRS[d]
        src, dst = (fz.at[d, s], rz.at[d, s]) if dy == 0 else (fy.at[s], ry.at[d - 2, s])
        return remote(src, dst, base_ring + s * 4 + d, target(dz, dy))

    def adj_z(t, p, d):
        at = slice(p * BS, (p + 1) * BS)
        return remote(
            az.at[d, t, at], azr.at[d, t, at], base_az + t * one_z + d * parts + p, target(*DIRS[d]))

    def adj(t, d):
        dz, dy = DIRS[d]
        row = 0 if dz < 0 else (zb_n + 1 if dz > 0 else None)
        if dz == 0:
            src, dst = oy.at[d - 2, t, :, BS:BS + cells_z, :], oyr.at[d - 2, t]
        else:
            src = oy.at[0 if dy < 0 else 1, t, :, row * BS:(row + 1) * BS, :]
            dst = ocr.at[d - 4, t]
        return remote(src, dst, base_ay + t * 6 + d - 2, target(dz, dy))

    follow_copy = remote(vol_in.at[0], nxt, base_p, previous)
    frac_copy = remote(fracs.at[phases], fracs.at[0], base_p + 1, following)
    first_zb = jnp.where((me_z > 0), zb_n - 1, 0)
    stages = [lax.rem(first_zb + i, zb_n) for i in range(zb_n)]

    def ring_on(d):
        return remote(rz.at[d, phases], rz.at[d, 0], base_p + 2 + rows + d, following)

    def passed(d):
        return exists(-DIRS[d][0], 0)

    def source_copy(i, xb):
        zs = pl.ds(pl.multiple_of(stages[i] * BS, BS), BS)
        xs = slice(xb * BS, (xb + 1) * BS)
        return remote(gath.at[phases, xs, zs, :], gath.at[0, xs, zs, :], base_p + 2 + i * xb_n + xb, following)

    def start(make, ds):
        for d in ds:
            pl.when(exists(*DIRS[d]))(lambda d=d: make(d).start())

    def arrive(make, ds):
        for d in ds:
            dz, dy = DIRS[d]
            pl.when(exists(-dz, -dy))(lambda d=d: make(d).wait_recv())

    def sent(make, ds):
        for d in ds:
            pl.when(exists(*DIRS[d]))(lambda d=d: make(d).wait_send())

    fetch = pltpu.make_async_copy(vol_in, vol, lsem.at[0])
    fetch.start()
    barrier = pltpu.get_barrier_semaphore()
    count = 2
    for d in range(8):
        here = exists(*DIRS[d])
        count = count + here.astype(jnp.int32)

        @pl.when(here)
        def _(d=d):
            pl.semaphore_signal(barrier, inc=1, device_id=target(*DIRS[d]), device_id_type=MESH)

    for where in (following, previous):
        pl.semaphore_signal(barrier, inc=1, device_id=where, device_id_type=MESH)
    lane = lax.broadcasted_iota(jnp.int32, (BS, cells_y), 1)
    sub = lax.broadcasted_iota(jnp.int32, (BS, cells_y), 0)
    lane_blk = lane // BS
    lane_half = lane_blk.astype(F32).astype(BF16)
    row_of = lax.broadcasted_iota(jnp.int32, (rows, cells_y), 0)
    row_blk = lax.broadcasted_iota(jnp.int32, (rows, cells_y), 1) // BS
    lane_in = lane - lane_blk * BS
    lane_z = lax.broadcasted_iota(jnp.int32, (cells_z, cells_y), 1)
    blk_z = lane_z // BS

    pl.semaphore_wait(barrier, count)
    follow_copy.start()
    for p in range(parts):
        start(functools.partial(halo_z, 0, p), range(2))
    fetch.wait()
    for t in range(phases):
        def pack(q, carry, t=t):
            lo = jnp.zeros((cells_z, cells_y), F32)
            hi = jnp.zeros((cells_z, cells_y), F32)
            for xb in range(xb_n):
                for j in range(per):
                    k = xb * per + j
                    plane = vol[t, xb * BS + q * per + j].astype(F32)
                    lo = jnp.where(blk_z == k, roll(plane, BS * k, 1), lo)
                    hi = jnp.where(blk_z == k, roll(plane, BS * k + BS, 1), hi)
            pk[0, t, q] = lo.astype(BF16)
            pk[1, t, q] = hi.astype(BF16)
            return carry

        lax.fori_loop(0, quads, pack, 0)
        start(functools.partial(halo, t), (2, 3))

    for t in range(phases):
        start(functools.partial(corner, t), range(4, 8))
    for t in range(1, phases):
        for p in range(EARLY_HALO):
            start(functools.partial(halo_z, t, p), range(2))

    for t in range(phases):
        c = jnp.zeros((rows, cells_y), jnp.int32)
        f = jnp.zeros((rows, cells_y), jnp.int32)
        for row in range(rows):
            cr = jnp.zeros((1, cells_y), jnp.int32)
            fr = jnp.zeros((1, cells_y), jnp.int32)
            for k in range(yb_n):
                cr = jnp.where(lane_blk[:1] == k, shift[t, row * yb_n + k], cr)
                fr = jnp.where(lane_blk[:1] == k, frac[t, row * yb_n + k], fr)
            c = jnp.where(row_of == row, cr, c)
            f = jnp.where(row_of == row, fr, f)
        one = lambda m: m.astype(jnp.int32)
        dx = one(c >= 9) + one(c >= 18)
        c = c - 9 * dx
        dz = one(c >= 3) + one(c >= 6)
        dy = c - 3 * dz
        bx, bz = row_of // zb_n, row_of % zb_n
        ex = jnp.clip(bx + dx - 1, 0, xb_n - 1) - bx + 1
        gz0 = me_z * zb_n + bz
        ez = jnp.clip(gz0 + dz - 1, 0, n_gz * zb_n - 1) - gz0 + 1
        gy0 = me_y * yb_n + row_blk
        ey = jnp.clip(gy0 + dy - 1, 0, n_gy * yb_n - 1) - gy0 + 1
        codes[t] = ex * 9 + ez * 3 + ey
        offs[t] = (ey * (zb_n + 2) + bz + ez) * cells_x + (bx + ex - 1) * BS
        for i, level in enumerate((f // 16, (f // 4) % 4, f % 4)):
            fracs[t + 1, i] = jnp.where(
                level == 0, F32(1 / 5), jnp.where(
                    level == 1, F32(2 / 5), jnp.where(level == 2, F32(3 / 5), F32(4 / 5))))
    frac_copy.start()
    place = pltpu.make_async_copy(offs, places, lsem.at[1])
    place.start()

    for d in range(8):
        dz, dy = DIRS[d]

        @pl.when(jnp.logical_not(exists(-dz, -dy)))
        def _(d=d, dz=dz, dy=dy):
            if dy == 0:
                rz[d] = jnp.zeros(rz.shape[1:], BF16)
                azr[d] = jnp.zeros(azr.shape[1:], BF16)
            elif dz == 0:
                ry[d - 2] = jnp.zeros(ry.shape[1:], F32)
                oyr[d - 2] = jnp.zeros(oyr.shape[1:], BF16)
            else:
                ocr[d - 4] = jnp.zeros(ocr.shape[1:], BF16)
    for s in range(phases + 1):
        resid[s, 0] = jnp.zeros((cells_z, cells_y), F32)
        resid[s, cells_x + 1] = jnp.zeros((cells_z, cells_y), F32)

    def widen(t, parts):
        def body(q, carry):
            for ze in parts:
                if ze == 0:
                    left, right = ch[7 - 4, t, q], ch[6 - 4, t, q]
                elif ze == zb_n + 1:
                    left, right = ch[5 - 4, t, q], ch[4 - 4, t, q]
                else:
                    at = slice((ze - 1) * BS, ze * BS)
                    left, right = yh[1, t, q, at, :], yh[0, t, q, at, :]
                left, right = left.astype(F32), right.astype(F32)
                for xb in range(xb_n):
                    for j in range(per):
                        k = xb * per + j
                        x = xb * BS + q * per + j
                        if ze == 0:
                            plane = zh[1, t, x]
                        elif ze == zb_n + 1:
                            plane = zh[0, t, x]
                        else:
                            plane = vol[t, x, (ze - 1) * BS:ze * BS, :]
                        wide[t, (zb_n + 2 + ze) * cells_x + x] = plane
                        plane = plane.astype(F32)
                        wide[t, ze * cells_x + x] = jnp.where(
                            lane < BS, roll(left, -BS * k, 1), roll(plane, BS, 1)).astype(BF16)
                        wide[t, (2 * zb_n + 4 + ze) * cells_x + x] = jnp.where(
                            lane >= cells_y - BS, roll(right, -BS - BS * k, 1), roll(plane, -BS, 1)).astype(BF16)
            return carry

        lax.fori_loop(0, quads, body, 0)

    def gather(t, zb, lo, hi):
        def body(xb, carry):
            row = xb * zb_n + zb
            acc = None
            for k in range(yb_n):
                cand = wide[t, pl.ds(places[t, row, k * BS], BS)]
                acc = cand if acc is None else jnp.where((lane_half == k)[None], cand, acc)
            xs = pl.ds(pl.multiple_of(xb * BS, BS), BS)
            zs = pl.ds(pl.multiple_of(zb * BS, BS), BS)
            gath[t + 1, xs, zs, :] = acc
            return carry

        lax.fori_loop(lo, hi, body, 0)

    def factors(s, row):
        fx, fz_, fy_ = (
            jnp.broadcast_to(fracs[s, i, pl.ds(row, 1), :], (BS, cells_y)) for i in range(3))
        return fx, jnp.where(sub == BS - 1, 0.0, fz_), jnp.where(lane_in == BS - 1, 0.0, fy_)

    def warp(s, zb, lo_x, hi_x):
        upcoming = vol.at[s] if s < phases else nxt

        def body(xb, carry):
            row = xb * zb_n + zb
            xs = pl.ds(pl.multiple_of(xb * BS, BS), BS)
            zs = pl.ds(pl.multiple_of(zb * BS, BS), BS)
            fx, fz_, fy_ = factors(s, row)
            v = gath[s, xs, zs, :].astype(F32)
            face = jnp.zeros((BS, cells_y), F32)
            for a in range(BS):
                p = v[a]
                if a < BS - 1:
                    p = p + fx * (v[a + 1] - p)
                p = p + fz_ * (roll(p, -1, 0) - p)
                p = p + fy_ * (roll(p, -1, 1) - p)
                p = p - upcoming[xb * BS + a, zs, :].astype(F32)
                resid[s, 1 + xb * BS + a, zs, :] = p
                face = jnp.where(lane // 2 == a, roll(p, 2 * a + 1, 1), face)
            fy[s, xb, zs, :] = face

            def z_face(side, z):
                fz[side, s, xs, :] = jnp.concatenate(
                    [resid[s, 1 + xb * BS + a, z:z + 1, :] for a in range(BS)], axis=0).astype(BF16)

            if s > 0:
                pl.when((zb == 0) & exists(-1, 0))(lambda: z_face(0, 0))
                pl.when((zb == zb_n - 1) & exists(1, 0))(lambda: z_face(1, cells_z - 1))

            return carry

        lax.fori_loop(lo_x, hi_x, body, 0)

    sub_z = lax.broadcasted_iota(jnp.int32, (cells_z, cells_y), 0)

    def smooth(s):
        if s == 0:
            for d in range(2):
                pl.when(passed(d))(lambda d=d: ring_on(d).wait_recv())
            arrive(functools.partial(ring, s), (2, 3))
        else:
            arrive(functools.partial(ring, s), range(4))
        if s == phases:
            for d in range(2):
                pl.when(passed(d))(lambda d=d: ring_on(d).start())
        w0, w1, w2, w3 = stencil[0], stencil[1], stencil[2], stencil[3]

        def body(xb, carry):
            sides = jnp.where(lane_z % 2 == 1, roll(ry[1, s, xb], 1, 1), roll(ry[0, s, xb], -1, 1))
            below = rz[1, s, pl.ds(pl.multiple_of(xb * BS, BS), BS), :].astype(F32)
            above = rz[0, s, pl.ds(pl.multiple_of(xb * BS, BS), BS), :].astype(F32)
            for a in range(BS):
                x = xb * BS + a
                c = resid[s, x + 1]
                along_x = resid[s, x] + resid[s, x + 2]
                up = jnp.where(sub_z == 0, jnp.broadcast_to(below[a:a + 1], c.shape), roll(c, 1, 0))
                dn = jnp.where(sub_z == cells_z - 1, jnp.broadcast_to(above[a:a + 1], c.shape), roll(c, -1, 0))
                ends = roll(sides, -2 * a - 1, 1)
                yl = jnp.where(lane_z == 0, ends, roll(c, 1, 1))
                yr = jnp.where(lane_z == cells_y - 1, ends, roll(c, -1, 1))
                total = w0 * c + w1 * along_x + w2 * (up + dn) + w3 * (yl + yr)
                if s == 0:
                    out[0, x] = out[0, x] - total
                else:
                    smo[s, x] = total
            return carry

        lax.fori_loop(0, xb_n, body, 0)

    def pull(t):
        def body(row, carry):
            xb, zb = row // zb_n, row % zb_n
            zs = pl.ds(pl.multiple_of(zb * BS, BS), BS)
            fx, fz_, fy_ = factors(t + 1, row)
            last = None
            for a in range(BS):
                p = smo[t + 1, xb * BS + a, zs, :]
                g = fz_ * p
                p = p - g + roll(g, 1, 0)
                g = fy_ * p
                p = p - g + roll(g, 1, 1)
                g = fx * p
                r = p if a == BS - 1 else p - g
                if last is not None:
                    r = r + last
                last = g
                pulled[t, xb * BS + a, zs, :] = r
            return carry

        lax.fori_loop(0, rows, body, 0)

    def scatter(t, parts):
        def body(q, carry):
            for ze in parts:
                pack_lo = jnp.zeros((BS, cells_y), F32)
                pack_hi = jnp.zeros((BS, cells_y), F32)
                for xs in range(xb_n):
                    accs = [jnp.zeros((per, BS, cells_y), F32) for _ in range(3)]
                    for dx in (-1, 0, 1):
                        for dz in (-1, 0, 1):
                            xd, zd = xs - dx, ze - 1 - dz
                            if not (0 <= xd < xb_n and 0 <= zd < zb_n):
                                continue
                            code = codes[t, pl.ds(xd * zb_n + zd, 1), :]
                            p = pulled[t, pl.ds(xd * BS + q * per, per), zd * BS:(zd + 1) * BS, :]
                            for dy in (-1, 0, 1):
                                hit = code == (dx + 1) * 9 + (dz + 1) * 3 + dy + 1
                                accs[dy + 1] = accs[dy + 1] + jnp.where(hit[None], p, 0.0)
                    for j in range(per):
                        k = xs * per + j
                        x = xs * BS + q * per + j
                        minus, zero, plus = accs[0][j], accs[1][j], accs[2][j]
                        total = (
                            zero
                            + jnp.where(lane >= BS, roll(plus, BS, 1), 0.0)
                            + jnp.where(lane < cells_y - BS, roll(minus, -BS, 1), 0.0)
                        )
                        pack_hi = jnp.where(lane_blk == k, roll(plus, BS + BS * k, 1), pack_hi)
                        pack_lo = jnp.where(lane_blk == k, roll(minus, BS * k, 1), pack_lo)
                        if ze == 0:
                            az[0, t, x] = total.astype(BF16)
                        elif ze == zb_n + 1:
                            az[1, t, x] = total.astype(BF16)
                        else:
                            own[t, x, (ze - 1) * BS:ze * BS, :] = total
                oy[0, t, q, ze * BS:(ze + 1) * BS, :] = pack_lo.astype(BF16)
                oy[1, t, q, ze * BS:(ze + 1) * BS, :] = pack_hi.astype(BF16)
            return carry

        lax.fori_loop(0, quads, body, 0)

    def finish(t):
        def body(q, carry):
            for zb in range(zb_n):
                at = slice(zb * BS, (zb + 1) * BS)
                left, right = oyr[1, t, q, at, :].astype(F32), oyr[0, t, q, at, :].astype(F32)
                for xb in range(xb_n):
                    for j in range(per):
                        k = xb * per + j
                        x = xb * BS + q * per + j
                        p = own[t, x, at, :]
                        p = p + jnp.where(lane < BS, roll(left, -BS * k, 1), 0.0)
                        p = p + jnp.where(lane >= cells_y - BS, roll(right, -BS - BS * k, 1), 0.0)
                        out[t, x, at, :] = p if t == 0 else p - smo[t, x, at, :]
            return carry

        lax.fori_loop(0, quads, body, 0)

    def finish_edge(t, side, zb, lo, hi):
        def body(q, carry):
            at = slice(zb * BS, (zb + 1) * BS)
            left, right = ocr[lo - 4, t, q].astype(F32), ocr[hi - 4, t, q].astype(F32)
            for xb in range(xb_n):
                for j in range(per):
                    k = xb * per + j
                    x = xb * BS + q * per + j
                    p = azr[side, t, x].astype(F32)
                    p = p + jnp.where(lane < BS, roll(left, -BS * k, 1), 0.0)
                    p = p + jnp.where(lane >= cells_y - BS, roll(right, -BS - BS * k, 1), 0.0)
                    out[t, x, at, :] = out[t, x, at, :] + p
            return carry

        lax.fori_loop(0, quads, body, 0)

    inner = range(1, zb_n + 1)

    def at_edges(work, t):
        pl.when(exists(-1, 0))(lambda: work(t, (0,)))
        pl.when(exists(1, 0))(lambda: work(t, (zb_n + 1,)))

    ends = ((0, -1, 1, 0, (6, 7)), (zb_n - 1, 1, 0, zb_n + 1, (4, 5)))

    def ready(t, i):
        for zb, dz, side, ze, ds in ends:
            @pl.when((stages[i] == zb) & exists(dz, 0))
            def _(side=side, ds=ds, ze=ze):
                for p in range(parts):
                    arrive(functools.partial(halo_z, t, p), (side,))
                arrive(functools.partial(corner, t), ds)
                widen(t, (ze,))

    def opening(t):
        arrive(functools.partial(halo, t), (2, 3))
        widen(t, inner)
        ready(t, 0)
        gather(t, stages[0], 0, xb_n)
        if t == last:
            for xb in range(xb_n):
                source_copy(0, xb).start()

    last = phases - 1
    for t in range(phases):
        if t == 0:
            place.wait()
            opening(t)
        if t < last:
            warp(t + 1, stages[0], 0, xb_n)
        for i in range(1, zb_n):
            ready(t, i)
            gather(t, stages[i], 0, xb_n)
            if t == last:
                for xb in range(xb_n):
                    source_copy(i, xb).start()
            else:
                warp(t + 1, stages[i], 0, xb_n)
        if t == last:
            follow_copy.wait_recv()
            for i in range(zb_n):
                warp(t + 1, stages[i], 0, xb_n)
        start(functools.partial(ring, t + 1), range(4))
        if t > 0:
            for p in range(EARLY_ADJ, parts):
                start(functools.partial(adj_z, t - 1, p), range(2))
            start(functools.partial(adj, t - 1), range(4, 8))
            scatter(t - 1, inner)
            start(functools.partial(adj, t - 1), (2, 3))
        if t < last:
            for p in range(EARLY_HALO, parts):
                start(functools.partial(halo_z, t + 1, p), range(2))
            opening(t + 1)
        smooth(t + 1)
        pull(t)
        at_edges(scatter, t)
        for p in range(EARLY_ADJ if t < last else parts):
            start(functools.partial(adj_z, t, p), range(2))
    scatter(last, inner)
    start(functools.partial(adj, last), (2, 3))

    def collect(t):
        for zb, dz, side, ze, ds in ends:
            @pl.when(exists(dz, 0))
            def _(zb=zb, side=side, ds=ds):
                for p in range(parts):
                    arrive(functools.partial(adj_z, t, p), (side,))
                arrive(functools.partial(adj, t), ds)
                finish_edge(t, side, zb, ds[1], ds[0])

    def settle(t):
        arrive(functools.partial(adj, t), (2, 3))
        finish(t)

    if last > 0:
        settle(0)
    frac_copy.wait_recv()
    for i in range(zb_n):
        for xb in range(xb_n):
            source_copy(i, xb).wait_recv()
        warp(0, stages[i], 0, xb_n)
    start(functools.partial(ring, 0), (2, 3))
    start(functools.partial(adj, last), range(4, 8))
    for t in range(min(1, last), phases):
        settle(t)
    for t in range(last):
        collect(t)
    smooth(0)
    collect(last)
    for t in range(phases):
        for p in range(parts):
            sent(functools.partial(halo_z, t, p), range(2))
            sent(functools.partial(adj_z, t, p), range(2))
        sent(functools.partial(halo, t), (2, 3))
        sent(functools.partial(corner, t), range(4, 8))
        sent(functools.partial(adj, t), range(2, 8))
    for s in range(phases + 1):
        sent(functools.partial(ring, s), range(4) if s > 0 else (2, 3))
    for d in range(2):
        pl.when(passed(d))(lambda d=d: ring_on(d).wait_send())
    for copy in (follow_copy, frac_copy, *(source_copy(i, xb) for i in range(zb_n) for xb in range(xb_n))):
        copy.wait_send()


def body(sizes, volume, shift_code, frac_code, stencil):
    t, x, z, y = volume.shape
    xb, zb, yb = x // BS, z // BS, y // BS
    quads = BS * xb // yb
    rows = xb * zb
    blocks = shift_code.shape[-1]
    n_sem = t * (4 * xb + 12) + 4 * (t + 1) + 4 + xb * zb
    V = pltpu.VMEM
    scratch = [
        V((t, x, z, y), BF16),
        V((x, z, y), BF16),
        V((2, t, x, BS, y), BF16),
        V((2, t, quads, z, y), BF16),
        V((4, t, quads, BS, y), BF16),
        V((2, t, quads, z, y), BF16),
        V((t, 3 * (zb + 2) * x, BS, y), BF16),
        V((t, rows, y), jnp.int32),
        V((t, rows, y), jnp.int32),
        pltpu.SMEM((t, rows, y), jnp.int32),
        V((t + 1, 3, rows, y), F32),
        V((t + 1, x, z, y), BF16),
        V((t + 1, x + 2, z, y), F32),
        V((2, t + 1, x, y), BF16),
        V((t + 1, xb, z, y), F32),
        V((2, t + 1, x, y), BF16),
        V((2, t + 1, xb, z, y), F32),
        V((t + 1, x, z, y), F32),
        V((t, x, z, y), F32),
        V((t, x, z, y), F32),
        V((2, t, x, BS, y), BF16),
        V((2, t, x, BS, y), BF16),
        V((2, t, quads, z + 2 * BS, y), BF16),
        V((2, t, quads, z, y), BF16),
        V((4, t, quads, BS, y), BF16),
        pltpu.SemaphoreType.DMA((n_sem,)),
        pltpu.SemaphoreType.DMA((n_sem,)),
        pltpu.SemaphoreType.DMA((2,)),
    ]
    vm, sm = pl.BlockSpec(memory_space=pltpu.VMEM), pl.BlockSpec(memory_space=pltpu.SMEM)
    return pl.pallas_call(
        functools.partial(kernel, sizes),
        out_shape=pltpu.VMEM((t, x, z, y), F32),
        in_specs=[pl.BlockSpec(memory_space=pl.ANY), sm, sm, sm],
        out_specs=vm,
        scratch_shapes=scratch,
        compiler_params=pltpu.CompilerParams(
            collective_id=0, has_side_effects=True, vmem_limit_bytes=60 * 1024 * 1024
        ),
    )(volume, shift_code.reshape(t, blocks), frac_code.reshape(t, blocks), stencil)


def solution(mesh):
    placed = (
        P("phase", None, "gz", "gy"),
        P("phase", "gz", "gy", None),
        P("phase", "gz", "gy", None),
        P(),
    )
    sizes = tuple(mesh.shape[name] for name in ("phase", "gz", "gy"))
    return jax.shard_map(
        functools.partial(body, sizes), mesh=mesh, in_specs=placed,
        out_specs=P("phase", None, "gz", "gy"), check_vma=False,
    )
```

```python
import functools

import jax
import jax.numpy as jnp
from jax import lax
from jax.experimental import pallas as pl
from jax.experimental.pallas import tpu as pltpu
from jax.sharding import PartitionSpec as P

BS = 16
EARLY_HALO = 2
EARLY_ADJ = 2
DIRS = ((-1, 0), (1, 0), (0, -1), (0, 1), (-1, -1), (-1, 1), (1, -1), (1, 1))
MESH = pl.DeviceIdType.MESH
F32 = jnp.float32
BF16 = jnp.bfloat16


def roll(x, shift, axis):
    size = x.shape[axis]
    shift = shift % size
    return x if shift == 0 else pltpu.roll(x, shift, axis)


def kernel(
    sizes, vol_in, shift, frac, stencil, out,
    vol, nxt, zh, yh, ch, pk, wide, codes, offs, places, fracs, gath, resid, fz, fy, rz, ry,
    smo, pulled, own, az, azr, oy, oyr, ocr, ssem, rsem, lsem,
):
    n_phase, n_gz, n_gy = sizes
    phases, cells_x, cells_z, cells_y = vol.shape
    xb_n, zb_n, yb_n = cells_x // BS, cells_z // BS, cells_y // BS
    per = yb_n // xb_n
    quads = BS // per
    rows = xb_n * zb_n
    me_p, me_z, me_y = lax.axis_index("phase"), lax.axis_index("gz"), lax.axis_index("gy")

    def exists(dz, dy):
        z, y = me_z + dz, me_y + dy
        return (z >= 0) & (z < n_gz) & (y >= 0) & (y < n_gy)

    def target(dz, dy):
        return {
            "gz": jnp.clip(me_z + dz, 0, n_gz - 1),
            "gy": jnp.clip(me_y + dy, 0, n_gy - 1),
        }

    following = {"phase": lax.rem(me_p + 1, n_phase)}
    previous = {"phase": lax.rem(me_p + n_phase - 1, n_phase)}

    def remote(src, dst, idx, where):
        return pltpu.make_async_remote_copy(
            src_ref=src, dst_ref=dst, send_sem=ssem.at[idx], recv_sem=rsem.at[idx],
            device_id=where, device_id_type=MESH,
        )

    parts = xb_n
    one_z = 2 * parts
    base_y = phases * one_z
    base_ring = base_y + 6 * phases
    base_az = base_ring + 4 * (phases + 1)
    base_ay = base_az + phases * one_z
    base_p = base_ay + 6 * phases

    def halo_z(t, p, d):
        dz, dy = DIRS[d]
        rows_z = slice(0, BS) if dz < 0 else slice(cells_z - BS, cells_z)
        at = slice(p * BS, (p + 1) * BS)
        return remote(
            vol_in.at[t, at, rows_z, :], zh.at[d, t, at], t * one_z + d * parts + p, target(dz, dy))

    def halo(t, d):
        return remote(pk.at[d - 2, t], yh.at[d - 2, t], base_y + t * 6 + d - 2, target(*DIRS[d]))

    def corner(t, d):
        dz, dy = DIRS[d]
        rows_z = slice(0, BS) if dz < 0 else slice(cells_z - BS, cells_z)
        return remote(
            pk.at[0 if dy < 0 else 1, t, :, rows_z, :], ch.at[d - 4, t],
            base_y + t * 6 + d - 2, target(dz, dy))

    def ring(s, d):
        dz, dy = DIRS[d]
        src, dst = (fz.at[d, s], rz.at[d, s]) if dy == 0 else (fy.at[s], ry.at[d - 2, s])
        return remote(src, dst, base_ring + s * 4 + d, target(dz, dy))

    def adj_z(t, p, d):
        at = slice(p * BS, (p + 1) * BS)
        return remote(
            az.at[d, t, at], azr.at[d, t, at], base_az + t * one_z + d * parts + p, target(*DIRS[d]))

    def adj(t, d):
        dz, dy = DIRS[d]
        row = 0 if dz < 0 else (zb_n + 1 if dz > 0 else None)
        if dz == 0:
            src, dst = oy.at[d - 2, t, :, BS:BS + cells_z, :], oyr.at[d - 2, t]
        else:
            src = oy.at[0 if dy < 0 else 1, t, :, row * BS:(row + 1) * BS, :]
            dst = ocr.at[d - 4, t]
        return remote(src, dst, base_ay + t * 6 + d - 2, target(dz, dy))

    follow_copy = remote(vol_in.at[0], nxt, base_p, previous)
    frac_copy = remote(fracs.at[phases], fracs.at[0], base_p + 1, following)
    first_zb = jnp.where((me_z > 0), zb_n - 1, 0)
    stages = [lax.rem(first_zb + i, zb_n) for i in range(zb_n)]

    def ring_on(d):
        return remote(rz.at[d, phases], rz.at[d, 0], base_p + 2 + rows + d, following)

    def passed(d):
        return exists(-DIRS[d][0], 0)

    def source_copy(i, xb):
        zs = pl.ds(pl.multiple_of(stages[i] * BS, BS), BS)
        xs = slice(xb * BS, (xb + 1) * BS)
        return remote(gath.at[phases, xs, zs, :], gath.at[0, xs, zs, :], base_p + 2 + i * xb_n + xb, following)

    def start(make, ds):
        for d in ds:
            pl.when(exists(*DIRS[d]))(lambda d=d: make(d).start())

    def arrive(make, ds):
        for d in ds:
            dz, dy = DIRS[d]
            pl.when(exists(-dz, -dy))(lambda d=d: make(d).wait_recv())

    def sent(make, ds):
        for d in ds:
            pl.when(exists(*DIRS[d]))(lambda d=d: make(d).wait_send())

    fetch = pltpu.make_async_copy(vol_in, vol, lsem.at[0])
    fetch.start()
    barrier = pltpu.get_barrier_semaphore()
    count = 2
    for d in range(8):
        here = exists(*DIRS[d])
        count = count + here.astype(jnp.int32)

        @pl.when(here)
        def _(d=d):
            pl.semaphore_signal(barrier, inc=1, device_id=target(*DIRS[d]), device_id_type=MESH)

    for where in (following, previous):
        pl.semaphore_signal(barrier, inc=1, device_id=where, device_id_type=MESH)
    lane = lax.broadcasted_iota(jnp.int32, (BS, cells_y), 1)
    sub = lax.broadcasted_iota(jnp.int32, (BS, cells_y), 0)
    lane_blk = lane // BS
    lane_half = lane_blk.astype(F32).astype(BF16)
    row_of = lax.broadcasted_iota(jnp.int32, (rows, cells_y), 0)
    row_blk = lax.broadcasted_iota(jnp.int32, (rows, cells_y), 1) // BS
    lane_in = lane - lane_blk * BS
    lane_z = lax.broadcasted_iota(jnp.int32, (cells_z, cells_y), 1)
    blk_z = lane_z // BS

    pl.semaphore_wait(barrier, count)
    follow_copy.start()
    for p in range(parts):
        start(functools.partial(halo_z, 0, p), range(2))
    fetch.wait()
    for t in range(phases):
        def pack(q, carry, t=t):
            lo = jnp.zeros((cells_z, cells_y), F32)
            hi = jnp.zeros((cells_z, cells_y), F32)
            for xb in range(xb_n):
                for j in range(per):
                    k = xb * per + j
                    plane = vol[t, xb * BS + q * per + j].astype(F32)
                    lo = jnp.where(blk_z == k, roll(plane, BS * k, 1), lo)
                    hi = jnp.where(blk_z == k, roll(plane, BS * k + BS, 1), hi)
            pk[0, t, q] = lo.astype(BF16)
            pk[1, t, q] = hi.astype(BF16)
            return carry

        lax.fori_loop(0, quads, pack, 0)
        start(functools.partial(halo, t), (2, 3))

    for t in range(phases):
        start(functools.partial(corner, t), range(4, 8))
    for t in range(1, phases):
        for p in range(EARLY_HALO):
            start(functools.partial(halo_z, t, p), range(2))

    for t in range(phases):
        c = jnp.zeros((rows, cells_y), jnp.int32)
        f = jnp.zeros((rows, cells_y), jnp.int32)
        for row in range(rows):
            cr = jnp.zeros((1, cells_y), jnp.int32)
            fr = jnp.zeros((1, cells_y), jnp.int32)
            for k in range(yb_n):
                cr = jnp.where(lane_blk[:1] == k, shift[t, row * yb_n + k], cr)
                fr = jnp.where(lane_blk[:1] == k, frac[t, row * yb_n + k], fr)
            c = jnp.where(row_of == row, cr, c)
            f = jnp.where(row_of == row, fr, f)
        one = lambda m: m.astype(jnp.int32)
        dx = one(c >= 9) + one(c >= 18)
        c = c - 9 * dx
        dz = one(c >= 3) + one(c >= 6)
        dy = c - 3 * dz
        bx, bz = row_of // zb_n, row_of % zb_n
        ex = jnp.clip(bx + dx - 1, 0, xb_n - 1) - bx + 1
        gz0 = me_z * zb_n + bz
        ez = jnp.clip(gz0 + dz - 1, 0, n_gz * zb_n - 1) - gz0 + 1
        gy0 = me_y * yb_n + row_blk
        ey = jnp.clip(gy0 + dy - 1, 0, n_gy * yb_n - 1) - gy0 + 1
        codes[t] = ex * 9 + ez * 3 + ey
        offs[t] = (ey * (zb_n + 2) + bz + ez) * cells_x + (bx + ex - 1) * BS
        for i, level in enumerate((f // 16, (f // 4) % 4, f % 4)):
            fracs[t + 1, i] = jnp.where(
                level == 0, F32(1 / 5), jnp.where(
                    level == 1, F32(2 / 5), jnp.where(level == 2, F32(3 / 5), F32(4 / 5))))
    frac_copy.start()
    place = pltpu.make_async_copy(offs, places, lsem.at[1])
    place.start()

    for d in range(8):
        dz, dy = DIRS[d]

        @pl.when(jnp.logical_not(exists(-dz, -dy)))
        def _(d=d, dz=dz, dy=dy):
            if dy == 0:
                rz[d] = jnp.zeros(rz.shape[1:], BF16)
            elif dz == 0:
                ry[d - 2] = jnp.zeros(ry.shape[1:], F32)
                oyr[d - 2] = jnp.zeros(oyr.shape[1:], BF16)
            else:
                ocr[d - 4] = jnp.zeros(ocr.shape[1:], BF16)
    for s in range(phases + 1):
        resid[s, 0] = jnp.zeros((cells_z, cells_y), F32)
        resid[s, cells_x + 1] = jnp.zeros((cells_z, cells_y), F32)

    def widen(t, parts):
        def body(q, carry):
            for ze in parts:
                if ze == 0:
                    left, right = ch[7 - 4, t, q], ch[6 - 4, t, q]
                elif ze == zb_n + 1:
                    left, right = ch[5 - 4, t, q], ch[4 - 4, t, q]
                else:
                    at = slice((ze - 1) * BS, ze * BS)
                    left, right = yh[1, t, q, at, :], yh[0, t, q, at, :]
                left, right = left.astype(F32), right.astype(F32)
                for xb in range(xb_n):
                    for j in range(per):
                        k = xb * per + j
                        x = xb * BS + q * per + j
                        if ze == 0:
                            plane = zh[1, t, x]
                        elif ze == zb_n + 1:
                            plane = zh[0, t, x]
                        else:
                            plane = vol[t, x, (ze - 1) * BS:ze * BS, :]
                        wide[t, (zb_n + 2 + ze) * cells_x + x] = plane
                        plane = plane.astype(F32)
                        wide[t, ze * cells_x + x] = jnp.where(
                            lane < BS, roll(left, -BS * k, 1), roll(plane, BS, 1)).astype(BF16)
                        wide[t, (2 * zb_n + 4 + ze) * cells_x + x] = jnp.where(
                            lane >= cells_y - BS, roll(right, -BS - BS * k, 1), roll(plane, -BS, 1)).astype(BF16)
            return carry

        lax.fori_loop(0, quads, body, 0)

    def gather(t, zb, lo, hi):
        def body(xb, carry):
            row = xb * zb_n + zb
            acc = None
            for k in range(yb_n):
                cand = wide[t, pl.ds(places[t, row, k * BS], BS)]
                acc = cand if acc is None else jnp.where((lane_half == k)[None], cand, acc)
            xs = pl.ds(pl.multiple_of(xb * BS, BS), BS)
            zs = pl.ds(pl.multiple_of(zb * BS, BS), BS)
            gath[t + 1, xs, zs, :] = acc
            return carry

        lax.fori_loop(lo, hi, body, 0)

    def factors(s, row):
        fx, fz_, fy_ = (
            jnp.broadcast_to(fracs[s, i, pl.ds(row, 1), :], (BS, cells_y)) for i in range(3))
        return fx, jnp.where(sub == BS - 1, 0.0, fz_), jnp.where(lane_in == BS - 1, 0.0, fy_)

    def warp(s, zb, lo_x, hi_x):
        upcoming = vol.at[s] if s < phases else nxt

        def body(xb, carry):
            row = xb * zb_n + zb
            xs = pl.ds(pl.multiple_of(xb * BS, BS), BS)
            zs = pl.ds(pl.multiple_of(zb * BS, BS), BS)
            fx, fz_, fy_ = factors(s, row)
            v = gath[s, xs, zs, :].astype(F32)
            face = jnp.zeros((BS, cells_y), F32)
            for a in range(BS):
                p = v[a]
                if a < BS - 1:
                    p = p + fx * (v[a + 1] - p)
                p = p + fz_ * (roll(p, -1, 0) - p)
                p = p + fy_ * (roll(p, -1, 1) - p)
                p = p - upcoming[xb * BS + a, zs, :].astype(F32)
                resid[s, 1 + xb * BS + a, zs, :] = p
                face = jnp.where(lane // 2 == a, roll(p, 2 * a + 1, 1), face)
            fy[s, xb, zs, :] = face

            def z_face(side, z):
                fz[side, s, xs, :] = jnp.concatenate(
                    [resid[s, 1 + xb * BS + a, z:z + 1, :] for a in range(BS)], axis=0).astype(BF16)

            if s > 0:
                pl.when((zb == 0) & exists(-1, 0))(lambda: z_face(0, 0))
                pl.when((zb == zb_n - 1) & exists(1, 0))(lambda: z_face(1, cells_z - 1))

            return carry

        lax.fori_loop(lo_x, hi_x, body, 0)

    sub_z = lax.broadcasted_iota(jnp.int32, (cells_z, cells_y), 0)

    def smooth(s):
        if s == 0:
            for d in range(2):
                pl.when(passed(d))(lambda d=d: ring_on(d).wait_recv())
            arrive(functools.partial(ring, s), (2, 3))
        else:
            arrive(functools.partial(ring, s), range(4))
        if s == phases:
            for d in range(2):
                pl.when(passed(d))(lambda d=d: ring_on(d).start())
        w0, w1, w2, w3 = stencil[0], stencil[1], stencil[2], stencil[3]

        def body(xb, carry):
            sides = jnp.where(lane_z % 2 == 1, roll(ry[1, s, xb], 1, 1), roll(ry[0, s, xb], -1, 1))
            below = rz[1, s, pl.ds(pl.multiple_of(xb * BS, BS), BS), :].astype(F32)
            above = rz[0, s, pl.ds(pl.multiple_of(xb * BS, BS), BS), :].astype(F32)
            for a in range(BS):
                x = xb * BS + a
                c = resid[s, x + 1]
                along_x = resid[s, x] + resid[s, x + 2]
                up = jnp.where(sub_z == 0, jnp.broadcast_to(below[a:a + 1], c.shape), roll(c, 1, 0))
                dn = jnp.where(sub_z == cells_z - 1, jnp.broadcast_to(above[a:a + 1], c.shape), roll(c, -1, 0))
                ends = roll(sides, -2 * a - 1, 1)
                yl = jnp.where(lane_z == 0, ends, roll(c, 1, 1))
                yr = jnp.where(lane_z == cells_y - 1, ends, roll(c, -1, 1))
                total = w0 * c + w1 * along_x + w2 * (up + dn) + w3 * (yl + yr)
                if s == 0:
                    out[0, x] = out[0, x] - total
                else:
                    smo[s, x] = total
            return carry

        lax.fori_loop(0, xb_n, body, 0)

    def pull(t):
        def body(row, carry):
            xb, zb = row // zb_n, row % zb_n
            zs = pl.ds(pl.multiple_of(zb * BS, BS), BS)
            fx, fz_, fy_ = factors(t + 1, row)
            last = None
            for a in range(BS):
                p = smo[t + 1, xb * BS + a, zs, :]
                g = fz_ * p
                p = p - g + roll(g, 1, 0)
                g = fy_ * p
                p = p - g + roll(g, 1, 1)
                g = fx * p
                r = p if a == BS - 1 else p - g
                if last is not None:
                    r = r + last
                last = g
                pulled[t, xb * BS + a, zs, :] = r
            return carry

        lax.fori_loop(0, rows, body, 0)

    def scatter(t, parts):
        def body(q, carry):
            for ze in parts:
                pack_lo = jnp.zeros((BS, cells_y), F32)
                pack_hi = jnp.zeros((BS, cells_y), F32)
                for xs in range(xb_n):
                    accs = [jnp.zeros((per, BS, cells_y), F32) for _ in range(3)]
                    for dx in (-1, 0, 1):
                        for dz in (-1, 0, 1):
                            xd, zd = xs - dx, ze - 1 - dz
                            if not (0 <= xd < xb_n and 0 <= zd < zb_n):
                                continue
                            code = codes[t, pl.ds(xd * zb_n + zd, 1), :]
                            p = pulled[t, pl.ds(xd * BS + q * per, per), zd * BS:(zd + 1) * BS, :]
                            for dy in (-1, 0, 1):
                                hit = code == (dx + 1) * 9 + (dz + 1) * 3 + dy + 1
                                accs[dy + 1] = accs[dy + 1] + jnp.where(hit[None], p, 0.0)
                    for j in range(per):
                        k = xs * per + j
                        x = xs * BS + q * per + j
                        minus, zero, plus = accs[0][j], accs[1][j], accs[2][j]
                        total = (
                            zero
                            + jnp.where(lane >= BS, roll(plus, BS, 1), 0.0)
                            + jnp.where(lane < cells_y - BS, roll(minus, -BS, 1), 0.0)
                        )
                        pack_hi = jnp.where(lane_blk == k, roll(plus, BS + BS * k, 1), pack_hi)
                        pack_lo = jnp.where(lane_blk == k, roll(minus, BS * k, 1), pack_lo)
                        if ze == 0:
                            az[0, t, x] = total.astype(BF16)
                        elif ze == zb_n + 1:
                            az[1, t, x] = total.astype(BF16)
                        else:
                            own[t, x, (ze - 1) * BS:ze * BS, :] = total
                oy[0, t, q, ze * BS:(ze + 1) * BS, :] = pack_lo.astype(BF16)
                oy[1, t, q, ze * BS:(ze + 1) * BS, :] = pack_hi.astype(BF16)
            return carry

        lax.fori_loop(0, quads, body, 0)

    def finish(t):
        def body(q, carry):
            for zb in range(zb_n):
                at = slice(zb * BS, (zb + 1) * BS)
                left, right = oyr[1, t, q, at, :].astype(F32), oyr[0, t, q, at, :].astype(F32)
                for xb in range(xb_n):
                    for j in range(per):
                        k = xb * per + j
                        x = xb * BS + q * per + j
                        p = own[t, x, at, :]
                        p = p + jnp.where(lane < BS, roll(left, -BS * k, 1), 0.0)
                        p = p + jnp.where(lane >= cells_y - BS, roll(right, -BS - BS * k, 1), 0.0)
                        out[t, x, at, :] = p if t == 0 else p - smo[t, x, at, :]
            return carry

        lax.fori_loop(0, quads, body, 0)

    def finish_edge(t, side, zb, lo, hi):
        def body(q, carry):
            at = slice(zb * BS, (zb + 1) * BS)
            left, right = ocr[lo - 4, t, q].astype(F32), ocr[hi - 4, t, q].astype(F32)
            for xb in range(xb_n):
                for j in range(per):
                    k = xb * per + j
                    x = xb * BS + q * per + j
                    p = azr[side, t, x].astype(F32)
                    p = p + jnp.where(lane < BS, roll(left, -BS * k, 1), 0.0)
                    p = p + jnp.where(lane >= cells_y - BS, roll(right, -BS - BS * k, 1), 0.0)
                    out[t, x, at, :] = out[t, x, at, :] + p
            return carry

        lax.fori_loop(0, quads, body, 0)

    inner = range(1, zb_n + 1)

    def at_edges(work, t):
        pl.when(exists(-1, 0))(lambda: work(t, (0,)))
        pl.when(exists(1, 0))(lambda: work(t, (zb_n + 1,)))

    ends = ((0, -1, 1, 0, (6, 7)), (zb_n - 1, 1, 0, zb_n + 1, (4, 5)))

    def ready(t, i):
        for zb, dz, side, ze, ds in ends:
            @pl.when((stages[i] == zb) & exists(dz, 0))
            def _(side=side, ds=ds, ze=ze):
                for p in range(parts):
                    arrive(functools.partial(halo_z, t, p), (side,))
                arrive(functools.partial(corner, t), ds)
                widen(t, (ze,))

    def opening(t):
        arrive(functools.partial(halo, t), (2, 3))
        widen(t, inner)
        ready(t, 0)
        gather(t, stages[0], 0, xb_n)
        if t == last:
            for xb in range(xb_n):
                source_copy(0, xb).start()

    last = phases - 1
    for t in range(phases):
        if t == 0:
            place.wait()
            opening(t)
        if t < last:
            warp(t + 1, stages[0], 0, xb_n)
        for i in range(1, zb_n):
            ready(t, i)
            gather(t, stages[i], 0, xb_n)
            if t == last:
                for xb in range(xb_n):
                    source_copy(i, xb).start()
            else:
                warp(t + 1, stages[i], 0, xb_n)
        if t == last:
            follow_copy.wait_recv()
            for i in range(zb_n):
                warp(t + 1, stages[i], 0, xb_n)
        start(functools.partial(ring, t + 1), range(4))
        if t > 0:
            for p in range(EARLY_ADJ, parts):
                start(functools.partial(adj_z, t - 1, p), range(2))
            start(functools.partial(adj, t - 1), range(4, 8))
            scatter(t - 1, inner)
            start(functools.partial(adj, t - 1), (2, 3))
        if t < last:
            for p in range(EARLY_HALO, parts):
                start(functools.partial(halo_z, t + 1, p), range(2))
            opening(t + 1)
        smooth(t + 1)
        pull(t)
        at_edges(scatter, t)
        for p in range(EARLY_ADJ if t < last else parts):
            start(functools.partial(adj_z, t, p), range(2))
    scatter(last, inner)
    start(functools.partial(adj, last), (2, 3))

    def collect(t):
        for zb, dz, side, ze, ds in ends:
            @pl.when(exists(dz, 0))
            def _(zb=zb, side=side, ds=ds):
                for p in range(parts):
                    arrive(functools.partial(adj_z, t, p), (side,))
                arrive(functools.partial(adj, t), ds)
                finish_edge(t, side, zb, ds[1], ds[0])

    def settle(t):
        arrive(functools.partial(adj, t), (2, 3))
        finish(t)

    if last > 0:
        settle(0)
    frac_copy.wait_recv()
    for i in range(zb_n):
        for xb in range(xb_n):
            source_copy(i, xb).wait_recv()
        warp(0, stages[i], 0, xb_n)
    start(functools.partial(ring, 0), (2, 3))
    start(functools.partial(adj, last), range(4, 8))
    for t in range(min(1, last), phases):
        settle(t)
    for t in range(last):
        collect(t)
    smooth(0)
    collect(last)
    for t in range(phases):
        for p in range(parts):
            sent(functools.partial(halo_z, t, p), range(2))
            sent(functools.partial(adj_z, t, p), range(2))
        sent(functools.partial(halo, t), (2, 3))
        sent(functools.partial(corner, t), range(4, 8))
        sent(functools.partial(adj, t), range(2, 8))
    for s in range(phases + 1):
        sent(functools.partial(ring, s), range(4) if s > 0 else (2, 3))
    for d in range(2):
        pl.when(passed(d))(lambda d=d: ring_on(d).wait_send())
    for copy in (follow_copy, frac_copy, *(source_copy(i, xb) for i in range(zb_n) for xb in range(xb_n))):
        copy.wait_send()


def body(sizes, volume, shift_code, frac_code, stencil):
    t, x, z, y = volume.shape
    xb, zb, yb = x // BS, z // BS, y // BS
    quads = BS * xb // yb
    rows = xb * zb
    blocks = shift_code.shape[-1]
    n_sem = t * (4 * xb + 12) + 4 * (t + 1) + 4 + xb * zb
    V = pltpu.VMEM
    scratch = [
        V((t, x, z, y), BF16),
        V((x, z, y), BF16),
        V((2, t, x, BS, y), BF16),
        V((2, t, quads, z, y), BF16),
        V((4, t, quads, BS, y), BF16),
        V((2, t, quads, z, y), BF16),
        V((t, 3 * (zb + 2) * x, BS, y), BF16),
        V((t, rows, y), jnp.int32),
        V((t, rows, y), jnp.int32),
        pltpu.SMEM((t, rows, y), jnp.int32),
        V((t + 1, 3, rows, y), F32),
        V((t + 1, x, z, y), BF16),
        V((t + 1, x + 2, z, y), F32),
        V((2, t + 1, x, y), BF16),
        V((t + 1, xb, z, y), F32),
        V((2, t + 1, x, y), BF16),
        V((2, t + 1, xb, z, y), F32),
        V((t + 1, x, z, y), F32),
        V((t, x, z, y), F32),
        V((t, x, z, y), F32),
        V((2, t, x, BS, y), BF16),
        V((2, t, x, BS, y), BF16),
        V((2, t, quads, z + 2 * BS, y), BF16),
        V((2, t, quads, z, y), BF16),
        V((4, t, quads, BS, y), BF16),
        pltpu.SemaphoreType.DMA((n_sem,)),
        pltpu.SemaphoreType.DMA((n_sem,)),
        pltpu.SemaphoreType.DMA((2,)),
    ]
    vm, sm = pl.BlockSpec(memory_space=pltpu.VMEM), pl.BlockSpec(memory_space=pltpu.SMEM)
    return pl.pallas_call(
        functools.partial(kernel, sizes),
        out_shape=pltpu.VMEM((t, x, z, y), F32),
        in_specs=[pl.BlockSpec(memory_space=pl.ANY), sm, sm, sm],
        out_specs=vm,
        scratch_shapes=scratch,
        compiler_params=pltpu.CompilerParams(
            collective_id=0, has_side_effects=True, vmem_limit_bytes=60 * 1024 * 1024
        ),
    )(volume, shift_code.reshape(t, blocks), frac_code.reshape(t, blocks), stencil)


def solution(mesh):
    placed = (
        P("phase", None, "gz", "gy"),
        P("phase", "gz", "gy", None),
        P("phase", "gz", "gy", None),
        P(),
    )
    sizes = tuple(mesh.shape[name] for name in ("phase", "gz", "gy"))
    return jax.shard_map(
        functools.partial(body, sizes), mesh=mesh, in_specs=placed,
        out_specs=P("phase", None, "gz", "gy"), check_vma=False,
    )
```

```python
import functools

import jax
import jax.numpy as jnp
from jax import lax
from jax.experimental import pallas as pl
from jax.experimental.pallas import tpu as pltpu
from jax.sharding import PartitionSpec as P

BS = 16
PARTS = 2
EARLY_HALO = 1
EARLY_ADJ = 1
DIRS = ((-1, 0), (1, 0), (0, -1), (0, 1), (-1, -1), (-1, 1), (1, -1), (1, 1))
MESH = pl.DeviceIdType.MESH
F32 = jnp.float32
BF16 = jnp.bfloat16


def roll(x, shift, axis):
    size = x.shape[axis]
    shift = shift % size
    return x if shift == 0 else pltpu.roll(x, shift, axis)


def kernel(
    sizes, vol_in, shift, frac, stencil, out,
    vol, nxt, zh, yh, ch, pk, wide, codes, offs, places, fracs, gath, resid, fz, fy, rz, ry,
    smo, pulled, own, az, azr, oy, oyr, ocr, ssem, rsem, lsem,
):
    n_phase, n_gz, n_gy = sizes
    phases, cells_x, cells_z, cells_y = vol.shape
    xb_n, zb_n, yb_n = cells_x // BS, cells_z // BS, cells_y // BS
    per = yb_n // xb_n
    quads = BS // per
    rows = xb_n * zb_n
    me_p, me_z, me_y = lax.axis_index("phase"), lax.axis_index("gz"), lax.axis_index("gy")

    def exists(dz, dy):
        z, y = me_z + dz, me_y + dy
        return (z >= 0) & (z < n_gz) & (y >= 0) & (y < n_gy)

    def target(dz, dy):
        return {
            "gz": jnp.clip(me_z + dz, 0, n_gz - 1),
            "gy": jnp.clip(me_y + dy, 0, n_gy - 1),
        }

    following = {"phase": lax.rem(me_p + 1, n_phase)}
    previous = {"phase": lax.rem(me_p + n_phase - 1, n_phase)}

    def remote(src, dst, idx, where):
        return pltpu.make_async_remote_copy(
            src_ref=src, dst_ref=dst, send_sem=ssem.at[idx], recv_sem=rsem.at[idx],
            device_id=where, device_id_type=MESH,
        )

    parts = PARTS
    part = cells_x // parts
    one_z = 2 * parts
    base_y = phases * one_z
    base_ring = base_y + 6 * phases
    base_az = base_ring + 4 * (phases + 1)
    base_ay = base_az + phases * one_z
    base_p = base_ay + 6 * phases

    def halo_z(t, p, d):
        dz, dy = DIRS[d]
        rows_z = slice(0, BS) if dz < 0 else slice(cells_z - BS, cells_z)
        at = slice(p * part, (p + 1) * part)
        return remote(
            vol_in.at[t, at, rows_z, :], zh.at[d, t, at], t * one_z + d * parts + p, target(dz, dy))

    def halo(t, d):
        return remote(pk.at[d - 2, t], yh.at[d - 2, t], base_y + t * 6 + d - 2, target(*DIRS[d]))

    def corner(t, d):
        dz, dy = DIRS[d]
        rows_z = slice(0, BS) if dz < 0 else slice(cells_z - BS, cells_z)
        return remote(
            pk.at[0 if dy < 0 else 1, t, :, rows_z, :], ch.at[d - 4, t],
            base_y + t * 6 + d - 2, target(dz, dy))

    def ring(s, d):
        dz, dy = DIRS[d]
        src, dst = (fz.at[d, s], rz.at[d, s]) if dy == 0 else (fy.at[s], ry.at[d - 2, s])
        return remote(src, dst, base_ring + s * 4 + d, target(dz, dy))

    def adj_z(t, p, d):
        at = slice(p * part, (p + 1) * part)
        return remote(
            az.at[d, t, at], azr.at[d, t, at], base_az + t * one_z + d * parts + p, target(*DIRS[d]))

    def adj(t, d):
        dz, dy = DIRS[d]
        row = 0 if dz < 0 else (zb_n + 1 if dz > 0 else None)
        if dz == 0:
            src, dst = oy.at[d - 2, t, :, BS:BS + cells_z, :], oyr.at[d - 2, t]
        else:
            src = oy.at[0 if dy < 0 else 1, t, :, row * BS:(row + 1) * BS, :]
            dst = ocr.at[d - 4, t]
        return remote(src, dst, base_ay + t * 6 + d - 2, target(dz, dy))

    follow_copy = remote(vol_in.at[0], nxt, base_p, previous)
    frac_copy = remote(fracs.at[phases], fracs.at[0], base_p + 1, following)
    first_zb = jnp.where((me_z > 0), zb_n - 1, 0)
    stages = [lax.rem(first_zb + i, zb_n) for i in range(zb_n)]

    def ring_on(d):
        return remote(rz.at[d, phases], rz.at[d, 0], base_p + 2 + rows + d, following)

    def passed(d):
        return exists(-DIRS[d][0], 0)

    def source_copy(i):
        zs = pl.ds(pl.multiple_of(stages[i] * BS, BS), BS)
        return remote(gath.at[phases, :, zs, :], gath.at[0, :, zs, :], base_p + 2 + i, following)

    def start(make, ds):
        for d in ds:
            pl.when(exists(*DIRS[d]))(lambda d=d: make(d).start())

    def arrive(make, ds):
        for d in ds:
            dz, dy = DIRS[d]
            pl.when(exists(-dz, -dy))(lambda d=d: make(d).wait_recv())

    def sent(make, ds):
        for d in ds:
            pl.when(exists(*DIRS[d]))(lambda d=d: make(d).wait_send())

    fetch = pltpu.make_async_copy(vol_in, vol, lsem.at[0])
    fetch.start()
    barrier = pltpu.get_barrier_semaphore()
    count = 2
    for d in range(8):
        here = exists(*DIRS[d])
        count = count + here.astype(jnp.int32)

        @pl.when(here)
        def _(d=d):
            pl.semaphore_signal(barrier, inc=1, device_id=target(*DIRS[d]), device_id_type=MESH)

    for where in (following, previous):
        pl.semaphore_signal(barrier, inc=1, device_id=where, device_id_type=MESH)
    lane = lax.broadcasted_iota(jnp.int32, (BS, cells_y), 1)
    sub = lax.broadcasted_iota(jnp.int32, (BS, cells_y), 0)
    lane_blk = lane // BS
    lane_half = lane_blk.astype(F32).astype(BF16)
    row_of = lax.broadcasted_iota(jnp.int32, (rows, cells_y), 0)
    row_blk = lax.broadcasted_iota(jnp.int32, (rows, cells_y), 1) // BS
    lane_in = lane - lane_blk * BS
    lane_z = lax.broadcasted_iota(jnp.int32, (cells_z, cells_y), 1)
    blk_z = lane_z // BS

    pl.semaphore_wait(barrier, count)
    follow_copy.start()
    for p in range(parts):
        start(functools.partial(halo_z, 0, p), range(2))
    fetch.wait()
    for t in range(phases):
        def pack(q, carry, t=t):
            lo = jnp.zeros((cells_z, cells_y), F32)
            hi = jnp.zeros((cells_z, cells_y), F32)
            for xb in range(xb_n):
                for j in range(per):
                    k = xb * per + j
                    plane = vol[t, xb * BS + q * per + j].astype(F32)
                    lo = jnp.where(blk_z == k, roll(plane, BS * k, 1), lo)
                    hi = jnp.where(blk_z == k, roll(plane, BS * k + BS, 1), hi)
            pk[0, t, q] = lo.astype(BF16)
            pk[1, t, q] = hi.astype(BF16)
            return carry

        lax.fori_loop(0, quads, pack, 0)
        start(functools.partial(halo, t), (2, 3))

    for t in range(phases):
        start(functools.partial(corner, t), range(4, 8))
    for t in range(1, phases):
        for p in range(EARLY_HALO):
            start(functools.partial(halo_z, t, p), range(2))

    for t in range(phases):
        c = jnp.zeros((rows, cells_y), jnp.int32)
        f = jnp.zeros((rows, cells_y), jnp.int32)
        for row in range(rows):
            cr = jnp.zeros((1, cells_y), jnp.int32)
            fr = jnp.zeros((1, cells_y), jnp.int32)
            for k in range(yb_n):
                cr = jnp.where(lane_blk[:1] == k, shift[t, row * yb_n + k], cr)
                fr = jnp.where(lane_blk[:1] == k, frac[t, row * yb_n + k], fr)
            c = jnp.where(row_of == row, cr, c)
            f = jnp.where(row_of == row, fr, f)
        one = lambda m: m.astype(jnp.int32)
        dx = one(c >= 9) + one(c >= 18)
        c = c - 9 * dx
        dz = one(c >= 3) + one(c >= 6)
        dy = c - 3 * dz
        bx, bz = row_of // zb_n, row_of % zb_n
        ex = jnp.clip(bx + dx - 1, 0, xb_n - 1) - bx + 1
        gz0 = me_z * zb_n + bz
        ez = jnp.clip(gz0 + dz - 1, 0, n_gz * zb_n - 1) - gz0 + 1
        gy0 = me_y * yb_n + row_blk
        ey = jnp.clip(gy0 + dy - 1, 0, n_gy * yb_n - 1) - gy0 + 1
        codes[t] = ex * 9 + ez * 3 + ey
        offs[t] = (ey * (zb_n + 2) + bz + ez) * cells_x + (bx + ex - 1) * BS
        for i, level in enumerate((f // 16, (f // 4) % 4, f % 4)):
            fracs[t + 1, i] = jnp.where(
                level == 0, F32(1 / 5), jnp.where(
                    level == 1, F32(2 / 5), jnp.where(level == 2, F32(3 / 5), F32(4 / 5))))
    frac_copy.start()
    place = pltpu.make_async_copy(offs, places, lsem.at[1])
    place.start()

    for d in range(8):
        dz, dy = DIRS[d]

        @pl.when(jnp.logical_not(exists(-dz, -dy)))
        def _(d=d, dz=dz, dy=dy):
            if dy == 0:
                rz[d] = jnp.zeros(rz.shape[1:], BF16)
            elif dz == 0:
                ry[d - 2] = jnp.zeros(ry.shape[1:], BF16)
                oyr[d - 2] = jnp.zeros(oyr.shape[1:], BF16)
            else:
                ocr[d - 4] = jnp.zeros(ocr.shape[1:], BF16)
    for s in range(phases + 1):
        resid[s, 0] = jnp.zeros((cells_z, cells_y), F32)
        resid[s, cells_x + 1] = jnp.zeros((cells_z, cells_y), F32)

    def widen(t, parts):
        def body(q, carry):
            for ze in parts:
                if ze == 0:
                    left, right = ch[7 - 4, t, q], ch[6 - 4, t, q]
                elif ze == zb_n + 1:
                    left, right = ch[5 - 4, t, q], ch[4 - 4, t, q]
                else:
                    at = slice((ze - 1) * BS, ze * BS)
                    left, right = yh[1, t, q, at, :], yh[0, t, q, at, :]
                left, right = left.astype(F32), right.astype(F32)
                for xb in range(xb_n):
                    for j in range(per):
                        k = xb * per + j
                        x = xb * BS + q * per + j
                        if ze == 0:
                            plane = zh[1, t, x]
                        elif ze == zb_n + 1:
                            plane = zh[0, t, x]
                        else:
                            plane = vol[t, x, (ze - 1) * BS:ze * BS, :]
                        wide[t, (zb_n + 2 + ze) * cells_x + x] = plane
                        plane = plane.astype(F32)
                        wide[t, ze * cells_x + x] = jnp.where(
                            lane < BS, roll(left, -BS * k, 1), roll(plane, BS, 1)).astype(BF16)
                        wide[t, (2 * zb_n + 4 + ze) * cells_x + x] = jnp.where(
                            lane >= cells_y - BS, roll(right, -BS - BS * k, 1), roll(plane, -BS, 1)).astype(BF16)
            return carry

        lax.fori_loop(0, quads, body, 0)

    def gather(t, zb, lo, hi):
        def body(xb, carry):
            row = xb * zb_n + zb
            acc = None
            for k in range(yb_n):
                cand = wide[t, pl.ds(places[t, row, k * BS], BS)]
                acc = cand if acc is None else jnp.where((lane_half == k)[None], cand, acc)
            xs = pl.ds(pl.multiple_of(xb * BS, BS), BS)
            zs = pl.ds(pl.multiple_of(zb * BS, BS), BS)
            gath[t + 1, xs, zs, :] = acc
            return carry

        lax.fori_loop(lo, hi, body, 0)

    def factors(s, row):
        fx, fz_, fy_ = (
            jnp.broadcast_to(fracs[s, i, pl.ds(row, 1), :], (BS, cells_y)) for i in range(3))
        return fx, jnp.where(sub == BS - 1, 0.0, fz_), jnp.where(lane_in == BS - 1, 0.0, fy_)

    def warp(s, zb, lo_x, hi_x):
        upcoming = vol.at[s] if s < phases else nxt

        def body(xb, carry):
            row = xb * zb_n + zb
            xs = pl.ds(pl.multiple_of(xb * BS, BS), BS)
            zs = pl.ds(pl.multiple_of(zb * BS, BS), BS)
            fx, fz_, fy_ = factors(s, row)
            v = gath[s, xs, zs, :].astype(F32)
            face = jnp.zeros((BS, cells_y), F32)
            for a in range(BS):
                p = v[a]
                if a < BS - 1:
                    p = p + fx * (v[a + 1] - p)
                p = p + fz_ * (roll(p, -1, 0) - p)
                p = p + fy_ * (roll(p, -1, 1) - p)
                p = p - upcoming[xb * BS + a, zs, :].astype(F32)
                resid[s, 1 + xb * BS + a, zs, :] = p
                face = jnp.where(lane // 2 == a, roll(p, 2 * a + 1, 1), face)
            fy[s, xb, zs, :] = face.astype(BF16)

            def z_face(side, z):
                fz[side, s, xs, :] = jnp.concatenate(
                    [resid[s, 1 + xb * BS + a, z:z + 1, :] for a in range(BS)], axis=0).astype(BF16)

            if s > 0:
                pl.when((zb == 0) & exists(-1, 0))(lambda: z_face(0, 0))
                pl.when((zb == zb_n - 1) & exists(1, 0))(lambda: z_face(1, cells_z - 1))

            return carry

        lax.fori_loop(lo_x, hi_x, body, 0)

    sub_z = lax.broadcasted_iota(jnp.int32, (cells_z, cells_y), 0)

    def smooth(s):
        if s == 0:
            for d in range(2):
                pl.when(passed(d))(lambda d=d: ring_on(d).wait_recv())
            arrive(functools.partial(ring, s), (2, 3))
        else:
            arrive(functools.partial(ring, s), range(4))
        if s == phases:
            for d in range(2):
                pl.when(passed(d))(lambda d=d: ring_on(d).start())
        w0, w1, w2, w3 = stencil[0], stencil[1], stencil[2], stencil[3]

        def body(xb, carry):
            sides = jnp.where(lane_z % 2 == 1, roll(ry[1, s, xb].astype(F32), 1, 1), roll(ry[0, s, xb].astype(F32), -1, 1))
            below = rz[1, s, pl.ds(pl.multiple_of(xb * BS, BS), BS), :].astype(F32)
            above = rz[0, s, pl.ds(pl.multiple_of(xb * BS, BS), BS), :].astype(F32)
            for a in range(BS):
                x = xb * BS + a
                c = resid[s, x + 1]
                along_x = resid[s, x] + resid[s, x + 2]
                up = jnp.where(sub_z == 0, jnp.broadcast_to(below[a:a + 1], c.shape), roll(c, 1, 0))
                dn = jnp.where(sub_z == cells_z - 1, jnp.broadcast_to(above[a:a + 1], c.shape), roll(c, -1, 0))
                ends = roll(sides, -2 * a - 1, 1)
                yl = jnp.where(lane_z == 0, ends, roll(c, 1, 1))
                yr = jnp.where(lane_z == cells_y - 1, ends, roll(c, -1, 1))
                total = w0 * c + w1 * along_x + w2 * (up + dn) + w3 * (yl + yr)
                if s == 0:
                    out[0, x] = out[0, x] - total
                else:
                    smo[s, x] = total
            return carry

        lax.fori_loop(0, xb_n, body, 0)

    def pull(t):
        def body(row, carry):
            xb, zb = row // zb_n, row % zb_n
            zs = pl.ds(pl.multiple_of(zb * BS, BS), BS)
            fx, fz_, fy_ = factors(t + 1, row)
            last = None
            for a in range(BS):
                p = smo[t + 1, xb * BS + a, zs, :]
                g = fz_ * p
                p = p - g + roll(g, 1, 0)
                g = fy_ * p
                p = p - g + roll(g, 1, 1)
                g = fx * p
                r = p if a == BS - 1 else p - g
                if last is not None:
                    r = r + last
                last = g
                pulled[t, xb * BS + a, zs, :] = r
            return carry

        lax.fori_loop(0, rows, body, 0)

    def scatter(t, parts):
        def body(q, carry):
            for ze in parts:
                pack_lo = jnp.zeros((BS, cells_y), F32)
                pack_hi = jnp.zeros((BS, cells_y), F32)
                for xs in range(xb_n):
                    accs = [jnp.zeros((per, BS, cells_y), F32) for _ in range(3)]
                    for dx in (-1, 0, 1):
                        for dz in (-1, 0, 1):
                            xd, zd = xs - dx, ze - 1 - dz
                            if not (0 <= xd < xb_n and 0 <= zd < zb_n):
                                continue
                            code = codes[t, pl.ds(xd * zb_n + zd, 1), :]
                            p = pulled[t, pl.ds(xd * BS + q * per, per), zd * BS:(zd + 1) * BS, :]
                            for dy in (-1, 0, 1):
                                hit = code == (dx + 1) * 9 + (dz + 1) * 3 + dy + 1
                                accs[dy + 1] = accs[dy + 1] + jnp.where(hit[None], p, 0.0)
                    for j in range(per):
                        k = xs * per + j
                        x = xs * BS + q * per + j
                        minus, zero, plus = accs[0][j], accs[1][j], accs[2][j]
                        total = (
                            zero
                            + jnp.where(lane >= BS, roll(plus, BS, 1), 0.0)
                            + jnp.where(lane < cells_y - BS, roll(minus, -BS, 1), 0.0)
                        )
                        pack_hi = jnp.where(lane_blk == k, roll(plus, BS + BS * k, 1), pack_hi)
                        pack_lo = jnp.where(lane_blk == k, roll(minus, BS * k, 1), pack_lo)
                        if ze == 0:
                            az[0, t, x] = total.astype(BF16)
                        elif ze == zb_n + 1:
                            az[1, t, x] = total.astype(BF16)
                        else:
                            own[t, x, (ze - 1) * BS:ze * BS, :] = total
                oy[0, t, q, ze * BS:(ze + 1) * BS, :] = pack_lo.astype(BF16)
                oy[1, t, q, ze * BS:(ze + 1) * BS, :] = pack_hi.astype(BF16)
            return carry

        lax.fori_loop(0, quads, body, 0)

    def finish(t):
        def body(q, carry):
            for zb in range(zb_n):
                at = slice(zb * BS, (zb + 1) * BS)
                left, right = oyr[1, t, q, at, :].astype(F32), oyr[0, t, q, at, :].astype(F32)
                for xb in range(xb_n):
                    for j in range(per):
                        k = xb * per + j
                        x = xb * BS + q * per + j
                        p = own[t, x, at, :]
                        p = p + jnp.where(lane < BS, roll(left, -BS * k, 1), 0.0)
                        p = p + jnp.where(lane >= cells_y - BS, roll(right, -BS - BS * k, 1), 0.0)
                        out[t, x, at, :] = p if t == 0 else p - smo[t, x, at, :]
            return carry

        lax.fori_loop(0, quads, body, 0)

    def finish_edge(t, side, zb, lo, hi):
        def body(q, carry):
            at = slice(zb * BS, (zb + 1) * BS)
            left, right = ocr[lo - 4, t, q].astype(F32), ocr[hi - 4, t, q].astype(F32)
            for xb in range(xb_n):
                for j in range(per):
                    k = xb * per + j
                    x = xb * BS + q * per + j
                    p = azr[side, t, x].astype(F32)
                    p = p + jnp.where(lane < BS, roll(left, -BS * k, 1), 0.0)
                    p = p + jnp.where(lane >= cells_y - BS, roll(right, -BS - BS * k, 1), 0.0)
                    out[t, x, at, :] = out[t, x, at, :] + p
            return carry

        lax.fori_loop(0, quads, body, 0)

    inner = range(1, zb_n + 1)

    def at_edges(work, t):
        pl.when(exists(-1, 0))(lambda: work(t, (0,)))
        pl.when(exists(1, 0))(lambda: work(t, (zb_n + 1,)))

    ends = ((0, -1, 1, 0, (6, 7)), (zb_n - 1, 1, 0, zb_n + 1, (4, 5)))

    def ready(t, i):
        for zb, dz, side, ze, ds in ends:
            @pl.when((stages[i] == zb) & exists(dz, 0))
            def _(side=side, ds=ds, ze=ze):
                for p in range(parts):
                    arrive(functools.partial(halo_z, t, p), (side,))
                arrive(functools.partial(corner, t), ds)
                widen(t, (ze,))

    def opening(t):
        arrive(functools.partial(halo, t), (2, 3))
        widen(t, inner)
        ready(t, 0)
        gather(t, stages[0], 0, xb_n)
        if t == last:
            source_copy(0).start()

    last = phases - 1
    for t in range(phases):
        if t == 0:
            place.wait()
            opening(t)
        if t < last:
            warp(t + 1, stages[0], 0, xb_n)
        for i in range(1, zb_n):
            ready(t, i)
            gather(t, stages[i], 0, xb_n)
            if t == last:
                source_copy(i).start()
            else:
                warp(t + 1, stages[i], 0, xb_n)
        if t == last:
            follow_copy.wait_recv()
            for i in range(zb_n):
                warp(t + 1, stages[i], 0, xb_n)
        start(functools.partial(ring, t + 1), range(4))
        if t > 0:
            for p in range(EARLY_ADJ, parts):
                start(functools.partial(adj_z, t - 1, p), range(2))
            start(functools.partial(adj, t - 1), range(4, 8))
            scatter(t - 1, inner)
            start(functools.partial(adj, t - 1), (2, 3))
        if t < last:
            for p in range(EARLY_HALO, parts):
                start(functools.partial(halo_z, t + 1, p), range(2))
            opening(t + 1)
        smooth(t + 1)
        pull(t)
        at_edges(scatter, t)
        for p in range(EARLY_ADJ if t < last else parts):
            start(functools.partial(adj_z, t, p), range(2))
    scatter(last, inner)
    start(functools.partial(adj, last), (2, 3))

    def collect(t):
        for zb, dz, side, ze, ds in ends:
            @pl.when(exists(dz, 0))
            def _(zb=zb, side=side, ds=ds):
                for p in range(parts):
                    arrive(functools.partial(adj_z, t, p), (side,))
                arrive(functools.partial(adj, t), ds)
                finish_edge(t, side, zb, ds[1], ds[0])

    def settle(t):
        arrive(functools.partial(adj, t), (2, 3))
        finish(t)

    if last > 0:
        settle(0)
    frac_copy.wait_recv()
    for i in range(zb_n):
        source_copy(i).wait_recv()
        warp(0, stages[i], 0, xb_n)
    start(functools.partial(ring, 0), (2, 3))
    start(functools.partial(adj, last), range(4, 8))
    for t in range(min(1, last), phases):
        settle(t)
    for t in range(last):
        collect(t)
    smooth(0)
    collect(last)
    for t in range(phases):
        for p in range(parts):
            sent(functools.partial(halo_z, t, p), range(2))
            sent(functools.partial(adj_z, t, p), range(2))
        sent(functools.partial(halo, t), (2, 3))
        sent(functools.partial(corner, t), range(4, 8))
        sent(functools.partial(adj, t), range(2, 8))
    for s in range(phases + 1):
        sent(functools.partial(ring, s), range(4) if s > 0 else (2, 3))
    for d in range(2):
        pl.when(passed(d))(lambda d=d: ring_on(d).wait_send())
    for copy in (follow_copy, frac_copy, *(source_copy(i) for i in range(zb_n))):
        copy.wait_send()


def body(sizes, volume, shift_code, frac_code, stencil):
    t, x, z, y = volume.shape
    xb, zb, yb = x // BS, z // BS, y // BS
    quads = BS * xb // yb
    rows = xb * zb
    blocks = shift_code.shape[-1]
    n_sem = t * (4 * PARTS + 12) + 4 * (t + 1) + 4 + xb * zb
    V = pltpu.VMEM
    scratch = [
        V((t, x, z, y), BF16),
        V((x, z, y), BF16),
        V((2, t, x, BS, y), BF16),
        V((2, t, quads, z, y), BF16),
        V((4, t, quads, BS, y), BF16),
        V((2, t, quads, z, y), BF16),
        V((t, 3 * (zb + 2) * x, BS, y), BF16),
        V((t, rows, y), jnp.int32),
        V((t, rows, y), jnp.int32),
        pltpu.SMEM((t, rows, y), jnp.int32),
        V((t + 1, 3, rows, y), F32),
        V((t + 1, x, z, y), BF16),
        V((t + 1, x + 2, z, y), F32),
        V((2, t + 1, x, y), BF16),
        V((t + 1, xb, z, y), BF16),
        V((2, t + 1, x, y), BF16),
        V((2, t + 1, xb, z, y), BF16),
        V((t + 1, x, z, y), F32),
        V((t, x, z, y), F32),
        V((t, x, z, y), F32),
        V((2, t, x, BS, y), BF16),
        V((2, t, x, BS, y), BF16),
        V((2, t, quads, z + 2 * BS, y), BF16),
        V((2, t, quads, z, y), BF16),
        V((4, t, quads, BS, y), BF16),
        pltpu.SemaphoreType.DMA((n_sem,)),
        pltpu.SemaphoreType.DMA((n_sem,)),
        pltpu.SemaphoreType.DMA((2,)),
    ]
    vm, sm = pl.BlockSpec(memory_space=pltpu.VMEM), pl.BlockSpec(memory_space=pltpu.SMEM)
    return pl.pallas_call(
        functools.partial(kernel, sizes),
        out_shape=pltpu.VMEM((t, x, z, y), F32),
        in_specs=[pl.BlockSpec(memory_space=pl.ANY), sm, sm, sm],
        out_specs=vm,
        scratch_shapes=scratch,
        compiler_params=pltpu.CompilerParams(
            collective_id=0, has_side_effects=True, vmem_limit_bytes=60 * 1024 * 1024
        ),
    )(volume, shift_code.reshape(t, blocks), frac_code.reshape(t, blocks), stencil)


def solution(mesh):
    placed = (
        P("phase", None, "gz", "gy"),
        P("phase", "gz", "gy", None),
        P("phase", "gz", "gy", None),
        P(),
    )
    sizes = tuple(mesh.shape[name] for name in ("phase", "gz", "gy"))
    return jax.shard_map(
        functools.partial(body, sizes), mesh=mesh, in_specs=placed,
        out_specs=P("phase", None, "gz", "gy"), check_vma=False,
    )
```

```python
import functools

import jax
import jax.numpy as jnp
from jax import lax
from jax.experimental import pallas as pl
from jax.experimental.pallas import tpu as pltpu
from jax.sharding import PartitionSpec as P

BS = 16
PARTS = 2
EARLY_HALO = 1
EARLY_ADJ = 1
DIRS = ((-1, 0), (1, 0), (0, -1), (0, 1), (-1, -1), (-1, 1), (1, -1), (1, 1))
MESH = pl.DeviceIdType.MESH
F32 = jnp.float32
BF16 = jnp.bfloat16


def roll(x, shift, axis):
    size = x.shape[axis]
    shift = shift % size
    return x if shift == 0 else pltpu.roll(x, shift, axis)


def kernel(
    sizes, vol_in, shift, frac, stencil, out,
    vol, nxt, zh, yh, ch, pk, wide, codes, offs, places, fracs, gath, resid, fz, fy, rz, ry,
    smo, pulled, own, az, azr, oy, oyr, ocr, ssem, rsem, lsem,
):
    n_phase, n_gz, n_gy = sizes
    phases, cells_x, cells_z, cells_y = vol.shape
    xb_n, zb_n, yb_n = cells_x // BS, cells_z // BS, cells_y // BS
    per = yb_n // xb_n
    quads = BS // per
    rows = xb_n * zb_n
    me_p, me_z, me_y = lax.axis_index("phase"), lax.axis_index("gz"), lax.axis_index("gy")

    def exists(dz, dy):
        z, y = me_z + dz, me_y + dy
        return (z >= 0) & (z < n_gz) & (y >= 0) & (y < n_gy)

    def target(dz, dy):
        return {
            "gz": jnp.clip(me_z + dz, 0, n_gz - 1),
            "gy": jnp.clip(me_y + dy, 0, n_gy - 1),
        }

    following = {"phase": lax.rem(me_p + 1, n_phase)}
    previous = {"phase": lax.rem(me_p + n_phase - 1, n_phase)}

    def remote(src, dst, idx, where):
        return pltpu.make_async_remote_copy(
            src_ref=src, dst_ref=dst, send_sem=ssem.at[idx], recv_sem=rsem.at[idx],
            device_id=where, device_id_type=MESH,
        )

    parts = PARTS
    part = cells_x // parts
    one_z = 2 * parts
    base_y = phases * one_z
    base_ring = base_y + 6 * phases
    base_az = base_ring + 4 * (phases + 1)
    base_ay = base_az + phases * one_z
    base_p = base_ay + 6 * phases

    def halo_z(t, p, d):
        dz, dy = DIRS[d]
        rows_z = slice(0, BS) if dz < 0 else slice(cells_z - BS, cells_z)
        at = slice(p * part, (p + 1) * part)
        return remote(
            vol_in.at[t, at, rows_z, :], zh.at[d, t, at], t * one_z + d * parts + p, target(dz, dy))

    def halo(t, d):
        return remote(pk.at[d - 2, t], yh.at[d - 2, t], base_y + t * 6 + d - 2, target(*DIRS[d]))

    def corner(t, d):
        dz, dy = DIRS[d]
        rows_z = slice(0, BS) if dz < 0 else slice(cells_z - BS, cells_z)
        return remote(
            pk.at[0 if dy < 0 else 1, t, :, rows_z, :], ch.at[d - 4, t],
            base_y + t * 6 + d - 2, target(dz, dy))

    def ring(s, d):
        dz, dy = DIRS[d]
        src, dst = (fz.at[d, s], rz.at[d, s]) if dy == 0 else (fy.at[s], ry.at[d - 2, s])
        return remote(src, dst, base_ring + s * 4 + d, target(dz, dy))

    def adj_z(t, p, d):
        at = slice(p * part, (p + 1) * part)
        return remote(
            az.at[d, t, at], azr.at[d, t, at], base_az + t * one_z + d * parts + p, target(*DIRS[d]))

    def adj(t, d):
        dz, dy = DIRS[d]
        row = 0 if dz < 0 else (zb_n + 1 if dz > 0 else None)
        if dz == 0:
            src, dst = oy.at[d - 2, t, :, BS:BS + cells_z, :], oyr.at[d - 2, t]
        else:
            src = oy.at[0 if dy < 0 else 1, t, :, row * BS:(row + 1) * BS, :]
            dst = ocr.at[d - 4, t]
        return remote(src, dst, base_ay + t * 6 + d - 2, target(dz, dy))

    follow_copy = remote(vol_in.at[0], nxt, base_p, previous)
    frac_copy = remote(fracs.at[phases], fracs.at[0], base_p + 1, following)
    first_zb = jnp.where((me_z > 0), zb_n - 1, 0)
    stages = [lax.rem(first_zb + i, zb_n) for i in range(zb_n)]

    def ring_on(d):
        return remote(rz.at[d, phases], rz.at[d, 0], base_p + 2 + rows + d, following)

    def passed(d):
        return exists(-DIRS[d][0], 0)

    def source_copy(i):
        zs = pl.ds(pl.multiple_of(stages[i] * BS, BS), BS)
        return remote(gath.at[phases, :, zs, :], gath.at[0, :, zs, :], base_p + 2 + i, following)

    def start(make, ds):
        for d in ds:
            pl.when(exists(*DIRS[d]))(lambda d=d: make(d).start())

    def arrive(make, ds):
        for d in ds:
            dz, dy = DIRS[d]
            pl.when(exists(-dz, -dy))(lambda d=d: make(d).wait_recv())

    def sent(make, ds):
        for d in ds:
            pl.when(exists(*DIRS[d]))(lambda d=d: make(d).wait_send())

    fetch = pltpu.make_async_copy(vol_in, vol, lsem.at[0])
    fetch.start()
    barrier = pltpu.get_barrier_semaphore()
    count = 2
    for d in range(8):
        here = exists(*DIRS[d])
        count = count + here.astype(jnp.int32)

        @pl.when(here)
        def _(d=d):
            pl.semaphore_signal(barrier, inc=1, device_id=target(*DIRS[d]), device_id_type=MESH)

    for where in (following, previous):
        pl.semaphore_signal(barrier, inc=1, device_id=where, device_id_type=MESH)
    lane = lax.broadcasted_iota(jnp.int32, (BS, cells_y), 1)
    sub = lax.broadcasted_iota(jnp.int32, (BS, cells_y), 0)
    lane_blk = lane // BS
    lane_half = lane_blk.astype(F32).astype(BF16)
    row_of = lax.broadcasted_iota(jnp.int32, (rows, cells_y), 0)
    row_blk = lax.broadcasted_iota(jnp.int32, (rows, cells_y), 1) // BS
    lane_in = lane - lane_blk * BS
    lane_z = lax.broadcasted_iota(jnp.int32, (cells_z, cells_y), 1)
    blk_z = lane_z // BS

    pl.semaphore_wait(barrier, count)
    follow_copy.start()
    for p in range(parts):
        start(functools.partial(halo_z, 0, p), range(2))
    fetch.wait()
    for t in range(phases):
        def pack(q, carry, t=t):
            lo = jnp.zeros((cells_z, cells_y), F32)
            hi = jnp.zeros((cells_z, cells_y), F32)
            for xb in range(xb_n):
                for j in range(per):
                    k = xb * per + j
                    plane = vol[t, xb * BS + q * per + j].astype(F32)
                    lo = jnp.where(blk_z == k, roll(plane, BS * k, 1), lo)
                    hi = jnp.where(blk_z == k, roll(plane, BS * k + BS, 1), hi)
            pk[0, t, q] = lo.astype(BF16)
            pk[1, t, q] = hi.astype(BF16)
            return carry

        lax.fori_loop(0, quads, pack, 0)
        start(functools.partial(halo, t), (2, 3))

    for t in range(phases):
        start(functools.partial(corner, t), range(4, 8))
    for t in range(1, phases):
        for p in range(EARLY_HALO):
            start(functools.partial(halo_z, t, p), range(2))

    for t in range(phases):
        c = jnp.zeros((rows, cells_y), jnp.int32)
        f = jnp.zeros((rows, cells_y), jnp.int32)
        for row in range(rows):
            cr = jnp.zeros((1, cells_y), jnp.int32)
            fr = jnp.zeros((1, cells_y), jnp.int32)
            for k in range(yb_n):
                cr = jnp.where(lane_blk[:1] == k, shift[t, row * yb_n + k], cr)
                fr = jnp.where(lane_blk[:1] == k, frac[t, row * yb_n + k], fr)
            c = jnp.where(row_of == row, cr, c)
            f = jnp.where(row_of == row, fr, f)
        one = lambda m: m.astype(jnp.int32)
        dx = one(c >= 9) + one(c >= 18)
        c = c - 9 * dx
        dz = one(c >= 3) + one(c >= 6)
        dy = c - 3 * dz
        bx, bz = row_of // zb_n, row_of % zb_n
        ex = jnp.clip(bx + dx - 1, 0, xb_n - 1) - bx + 1
        gz0 = me_z * zb_n + bz
        ez = jnp.clip(gz0 + dz - 1, 0, n_gz * zb_n - 1) - gz0 + 1
        gy0 = me_y * yb_n + row_blk
        ey = jnp.clip(gy0 + dy - 1, 0, n_gy * yb_n - 1) - gy0 + 1
        codes[t] = ex * 9 + ez * 3 + ey
        offs[t] = (ey * (zb_n + 2) + bz + ez) * cells_x + (bx + ex - 1) * BS
        for i, level in enumerate((f // 16, (f // 4) % 4, f % 4)):
            fracs[t + 1, i] = jnp.where(
                level == 0, F32(1 / 5), jnp.where(
                    level == 1, F32(2 / 5), jnp.where(level == 2, F32(3 / 5), F32(4 / 5))))
    frac_copy.start()
    place = pltpu.make_async_copy(offs, places, lsem.at[1])
    place.start()

    for d in range(8):
        dz, dy = DIRS[d]

        @pl.when(jnp.logical_not(exists(-dz, -dy)))
        def _(d=d, dz=dz, dy=dy):
            if dy == 0:
                rz[d] = jnp.zeros(rz.shape[1:], BF16)
            elif dz == 0:
                ry[d - 2] = jnp.zeros(ry.shape[1:], BF16)
                oyr[d - 2] = jnp.zeros(oyr.shape[1:], BF16)
            else:
                ocr[d - 4] = jnp.zeros(ocr.shape[1:], BF16)
    for s in range(phases + 1):
        resid[s, 0] = jnp.zeros((cells_z, cells_y), F32)
        resid[s, cells_x + 1] = jnp.zeros((cells_z, cells_y), F32)

    def widen(t, parts):
        def body(q, carry):
            for ze in parts:
                if ze == 0:
                    left, right = ch[7 - 4, t, q], ch[6 - 4, t, q]
                elif ze == zb_n + 1:
                    left, right = ch[5 - 4, t, q], ch[4 - 4, t, q]
                else:
                    at = slice((ze - 1) * BS, ze * BS)
                    left, right = yh[1, t, q, at, :], yh[0, t, q, at, :]
                left, right = left.astype(F32), right.astype(F32)
                for xb in range(xb_n):
                    for j in range(per):
                        k = xb * per + j
                        x = xb * BS + q * per + j
                        if ze == 0:
                            plane = zh[1, t, x]
                        elif ze == zb_n + 1:
                            plane = zh[0, t, x]
                        else:
                            plane = vol[t, x, (ze - 1) * BS:ze * BS, :]
                        wide[t, (zb_n + 2 + ze) * cells_x + x] = plane
                        plane = plane.astype(F32)
                        wide[t, ze * cells_x + x] = jnp.where(
                            lane < BS, roll(left, -BS * k, 1), roll(plane, BS, 1)).astype(BF16)
                        wide[t, (2 * zb_n + 4 + ze) * cells_x + x] = jnp.where(
                            lane >= cells_y - BS, roll(right, -BS - BS * k, 1), roll(plane, -BS, 1)).astype(BF16)
            return carry

        lax.fori_loop(0, quads, body, 0)

    def gather(t, zb, lo, hi):
        def body(xb, carry):
            row = xb * zb_n + zb
            acc = None
            for k in range(yb_n):
                cand = wide[t, pl.ds(places[t, row, k * BS], BS)]
                acc = cand if acc is None else jnp.where((lane_half == k)[None], cand, acc)
            xs = pl.ds(pl.multiple_of(xb * BS, BS), BS)
            zs = pl.ds(pl.multiple_of(zb * BS, BS), BS)
            gath[t + 1, xs, zs, :] = acc
            return carry

        lax.fori_loop(lo, hi, body, 0)

    def factors(s, row):
        fx, fz_, fy_ = (
            jnp.broadcast_to(fracs[s, i, pl.ds(row, 1), :], (BS, cells_y)) for i in range(3))
        return fx, jnp.where(sub == BS - 1, 0.0, fz_), jnp.where(lane_in == BS - 1, 0.0, fy_)

    def warp(s, zb, lo_x, hi_x):
        upcoming = vol.at[s] if s < phases else nxt

        def body(xb, carry):
            row = xb * zb_n + zb
            xs = pl.ds(pl.multiple_of(xb * BS, BS), BS)
            zs = pl.ds(pl.multiple_of(zb * BS, BS), BS)
            fx, fz_, fy_ = factors(s, row)
            v = gath[s, xs, zs, :].astype(F32)
            face = jnp.zeros((BS, cells_y), F32)
            for a in range(BS):
                p = v[a]
                if a < BS - 1:
                    p = p + fx * (v[a + 1] - p)
                p = p + fz_ * (roll(p, -1, 0) - p)
                p = p + fy_ * (roll(p, -1, 1) - p)
                p = p - upcoming[xb * BS + a, zs, :].astype(F32)
                resid[s, 1 + xb * BS + a, zs, :] = p
                face = jnp.where(lane // 2 == a, roll(p, 2 * a + 1, 1), face)
            fy[s, xb, zs, :] = face.astype(BF16)

            def z_face(side, z):
                fz[side, s, xs, :] = jnp.concatenate(
                    [resid[s, 1 + xb * BS + a, z:z + 1, :] for a in range(BS)], axis=0).astype(BF16)

            if s > 0:
                pl.when((zb == 0) & exists(-1, 0))(lambda: z_face(0, 0))
                pl.when((zb == zb_n - 1) & exists(1, 0))(lambda: z_face(1, cells_z - 1))

            return carry

        lax.fori_loop(lo_x, hi_x, body, 0)

    sub_z = lax.broadcasted_iota(jnp.int32, (cells_z, cells_y), 0)

    def smooth(s):
        if s == 0:
            for d in range(2):
                pl.when(passed(d))(lambda d=d: ring_on(d).wait_recv())
            arrive(functools.partial(ring, s), (2, 3))
        else:
            arrive(functools.partial(ring, s), range(4))
        if s == phases:
            for d in range(2):
                pl.when(passed(d))(lambda d=d: ring_on(d).start())
        w0, w1, w2, w3 = stencil[0], stencil[1], stencil[2], stencil[3]

        def body(xb, carry):
            sides = jnp.where(lane_z % 2 == 1, roll(ry[1, s, xb].astype(F32), 1, 1), roll(ry[0, s, xb].astype(F32), -1, 1))
            below = rz[1, s, pl.ds(pl.multiple_of(xb * BS, BS), BS), :].astype(F32)
            above = rz[0, s, pl.ds(pl.multiple_of(xb * BS, BS), BS), :].astype(F32)
            for a in range(BS):
                x = xb * BS + a
                c = resid[s, x + 1]
                along_x = resid[s, x] + resid[s, x + 2]
                up = jnp.where(sub_z == 0, jnp.broadcast_to(below[a:a + 1], c.shape), roll(c, 1, 0))
                dn = jnp.where(sub_z == cells_z - 1, jnp.broadcast_to(above[a:a + 1], c.shape), roll(c, -1, 0))
                ends = roll(sides, -2 * a - 1, 1)
                yl = jnp.where(lane_z == 0, ends, roll(c, 1, 1))
                yr = jnp.where(lane_z == cells_y - 1, ends, roll(c, -1, 1))
                total = w0 * c + w1 * along_x + w2 * (up + dn) + w3 * (yl + yr)
                if s == 0:
                    out[0, x] = out[0, x] - total
                else:
                    smo[s, x] = total
            return carry

        lax.fori_loop(0, xb_n, body, 0)

    def pull(t):
        def body(row, carry):
            xb, zb = row // zb_n, row % zb_n
            zs = pl.ds(pl.multiple_of(zb * BS, BS), BS)
            fx, fz_, fy_ = factors(t + 1, row)
            last = None
            for a in range(BS):
                p = smo[t + 1, xb * BS + a, zs, :]
                g = fz_ * p
                p = p - g + roll(g, 1, 0)
                g = fy_ * p
                p = p - g + roll(g, 1, 1)
                g = fx * p
                r = p if a == BS - 1 else p - g
                if last is not None:
                    r = r + last
                last = g
                pulled[t, xb * BS + a, zs, :] = r
            return carry

        lax.fori_loop(0, rows, body, 0)

    def scatter(t, parts):
        def body(q, carry):
            for ze in parts:
                pack_lo = jnp.zeros((BS, cells_y), F32)
                pack_hi = jnp.zeros((BS, cells_y), F32)
                for xs in range(xb_n):
                    accs = [jnp.zeros((per, BS, cells_y), F32) for _ in range(3)]
                    for dx in (-1, 0, 1):
                        for dz in (-1, 0, 1):
                            xd, zd = xs - dx, ze - 1 - dz
                            if not (0 <= xd < xb_n and 0 <= zd < zb_n):
                                continue
                            code = codes[t, pl.ds(xd * zb_n + zd, 1), :]
                            p = pulled[t, pl.ds(xd * BS + q * per, per), zd * BS:(zd + 1) * BS, :]
                            for dy in (-1, 0, 1):
                                hit = code == (dx + 1) * 9 + (dz + 1) * 3 + dy + 1
                                accs[dy + 1] = accs[dy + 1] + jnp.where(hit[None], p, 0.0)
                    for j in range(per):
                        k = xs * per + j
                        x = xs * BS + q * per + j
                        minus, zero, plus = accs[0][j], accs[1][j], accs[2][j]
                        total = (
                            zero
                            + jnp.where(lane >= BS, roll(plus, BS, 1), 0.0)
                            + jnp.where(lane < cells_y - BS, roll(minus, -BS, 1), 0.0)
                        )
                        pack_hi = jnp.where(lane_blk == k, roll(plus, BS + BS * k, 1), pack_hi)
                        pack_lo = jnp.where(lane_blk == k, roll(minus, BS * k, 1), pack_lo)
                        if ze == 0:
                            az[0, t, x] = total.astype(BF16)
                        elif ze == zb_n + 1:
                            az[1, t, x] = total.astype(BF16)
                        else:
                            own[t, x, (ze - 1) * BS:ze * BS, :] = total
                oy[0, t, q, ze * BS:(ze + 1) * BS, :] = pack_lo.astype(BF16)
                oy[1, t, q, ze * BS:(ze + 1) * BS, :] = pack_hi.astype(BF16)
            return carry

        lax.fori_loop(0, quads, body, 0)

    def finish(t):
        def body(q, carry):
            for zb in range(zb_n):
                at = slice(zb * BS, (zb + 1) * BS)
                left, right = oyr[1, t, q, at, :].astype(F32), oyr[0, t, q, at, :].astype(F32)
                for xb in range(xb_n):
                    for j in range(per):
                        k = xb * per + j
                        x = xb * BS + q * per + j
                        p = own[t, x, at, :]
                        p = p + jnp.where(lane < BS, roll(left, -BS * k, 1), 0.0)
                        p = p + jnp.where(lane >= cells_y - BS, roll(right, -BS - BS * k, 1), 0.0)
                        out[t, x, at, :] = p if t == 0 else p - smo[t, x, at, :]
            return carry

        lax.fori_loop(0, quads, body, 0)

    def finish_edge(t, side, zb, lo, hi):
        def body(q, carry):
            at = slice(zb * BS, (zb + 1) * BS)
            left, right = ocr[lo - 4, t, q].astype(F32), ocr[hi - 4, t, q].astype(F32)
            for xb in range(xb_n):
                for j in range(per):
                    k = xb * per + j
                    x = xb * BS + q * per + j
                    p = azr[side, t, x].astype(F32)
                    p = p + jnp.where(lane < BS, roll(left, -BS * k, 1), 0.0)
                    p = p + jnp.where(lane >= cells_y - BS, roll(right, -BS - BS * k, 1), 0.0)
                    out[t, x, at, :] = out[t, x, at, :] + p
            return carry

        lax.fori_loop(0, quads, body, 0)

    inner = range(1, zb_n + 1)

    def at_edges(work, t):
        pl.when(exists(-1, 0))(lambda: work(t, (0,)))
        pl.when(exists(1, 0))(lambda: work(t, (zb_n + 1,)))

    ends = ((0, -1, 1, 0, (6, 7)), (zb_n - 1, 1, 0, zb_n + 1, (4, 5)))

    def ready(t, i):
        for zb, dz, side, ze, ds in ends:
            @pl.when((stages[i] == zb) & exists(dz, 0))
            def _(side=side, ds=ds, ze=ze):
                for p in range(parts):
                    arrive(functools.partial(halo_z, t, p), (side,))
                arrive(functools.partial(corner, t), ds)
                widen(t, (ze,))

    def opening(t):
        arrive(functools.partial(halo, t), (2, 3))
        widen(t, inner)
        ready(t, 0)
        gather(t, stages[0], 0, xb_n)
        if t == last:
            source_copy(0).start()

    last = phases - 1
    for t in range(phases):
        if t == 0:
            place.wait()
            opening(t)
        if t < last:
            warp(t + 1, stages[0], 0, xb_n)
        else:
            follow_copy.wait_recv()
            warp(t + 1, stages[0], 0, xb_n)
        for i in range(1, zb_n):
            ready(t, i)
            gather(t, stages[i], 0, xb_n)
            if t == last:
                source_copy(i).start()
            else:
                warp(t + 1, stages[i], 0, xb_n)
        if t == last:
            for i in range(1, zb_n):
                warp(t + 1, stages[i], 0, xb_n)
        start(functools.partial(ring, t + 1), range(4))
        if t > 0:
            for p in range(EARLY_ADJ, parts):
                start(functools.partial(adj_z, t - 1, p), range(2))
            start(functools.partial(adj, t - 1), range(4, 8))
            scatter(t - 1, inner)
            start(functools.partial(adj, t - 1), (2, 3))
        if t < last:
            for p in range(EARLY_HALO, parts):
                start(functools.partial(halo_z, t + 1, p), range(2))
            opening(t + 1)
        smooth(t + 1)
        pull(t)
        at_edges(scatter, t)
        for p in range(EARLY_ADJ if t < last else parts):
            start(functools.partial(adj_z, t, p), range(2))
    scatter(last, inner)
    start(functools.partial(adj, last), (2, 3))

    def collect(t):
        for zb, dz, side, ze, ds in ends:
            @pl.when(exists(dz, 0))
            def _(zb=zb, side=side, ds=ds):
                for p in range(parts):
                    arrive(functools.partial(adj_z, t, p), (side,))
                arrive(functools.partial(adj, t), ds)
                finish_edge(t, side, zb, ds[1], ds[0])

    def settle(t):
        arrive(functools.partial(adj, t), (2, 3))
        finish(t)

    if last > 0:
        settle(0)
    frac_copy.wait_recv()
    for i in range(zb_n):
        source_copy(i).wait_recv()
        warp(0, stages[i], 0, xb_n)
    start(functools.partial(ring, 0), (2, 3))
    start(functools.partial(adj, last), range(4, 8))
    for t in range(min(1, last), phases):
        settle(t)
    for t in range(last):
        collect(t)
    smooth(0)
    collect(last)
    for t in range(phases):
        for p in range(parts):
            sent(functools.partial(halo_z, t, p), range(2))
            sent(functools.partial(adj_z, t, p), range(2))
        sent(functools.partial(halo, t), (2, 3))
        sent(functools.partial(corner, t), range(4, 8))
        sent(functools.partial(adj, t), range(2, 8))
    for s in range(phases + 1):
        sent(functools.partial(ring, s), range(4) if s > 0 else (2, 3))
    for d in range(2):
        pl.when(passed(d))(lambda d=d: ring_on(d).wait_send())
    for copy in (follow_copy, frac_copy, *(source_copy(i) for i in range(zb_n))):
        copy.wait_send()


def body(sizes, volume, shift_code, frac_code, stencil):
    t, x, z, y = volume.shape
    xb, zb, yb = x // BS, z // BS, y // BS
    quads = BS * xb // yb
    rows = xb * zb
    blocks = shift_code.shape[-1]
    n_sem = t * (4 * PARTS + 12) + 4 * (t + 1) + 4 + xb * zb
    V = pltpu.VMEM
    scratch = [
        V((t, x, z, y), BF16),
        V((x, z, y), BF16),
        V((2, t, x, BS, y), BF16),
        V((2, t, quads, z, y), BF16),
        V((4, t, quads, BS, y), BF16),
        V((2, t, quads, z, y), BF16),
        V((t, 3 * (zb + 2) * x, BS, y), BF16),
        V((t, rows, y), jnp.int32),
        V((t, rows, y), jnp.int32),
        pltpu.SMEM((t, rows, y), jnp.int32),
        V((t + 1, 3, rows, y), F32),
        V((t + 1, x, z, y), BF16),
        V((t + 1, x + 2, z, y), F32),
        V((2, t + 1, x, y), BF16),
        V((t + 1, xb, z, y), BF16),
        V((2, t + 1, x, y), BF16),
        V((2, t + 1, xb, z, y), BF16),
        V((t + 1, x, z, y), F32),
        V((t, x, z, y), F32),
        V((t, x, z, y), F32),
        V((2, t, x, BS, y), BF16),
        V((2, t, x, BS, y), BF16),
        V((2, t, quads, z + 2 * BS, y), BF16),
        V((2, t, quads, z, y), BF16),
        V((4, t, quads, BS, y), BF16),
        pltpu.SemaphoreType.DMA((n_sem,)),
        pltpu.SemaphoreType.DMA((n_sem,)),
        pltpu.SemaphoreType.DMA((2,)),
    ]
    vm, sm = pl.BlockSpec(memory_space=pltpu.VMEM), pl.BlockSpec(memory_space=pltpu.SMEM)
    return pl.pallas_call(
        functools.partial(kernel, sizes),
        out_shape=pltpu.VMEM((t, x, z, y), F32),
        in_specs=[pl.BlockSpec(memory_space=pl.ANY), sm, sm, sm],
        out_specs=vm,
        scratch_shapes=scratch,
        compiler_params=pltpu.CompilerParams(
            collective_id=0, has_side_effects=True, vmem_limit_bytes=60 * 1024 * 1024
        ),
    )(volume, shift_code.reshape(t, blocks), frac_code.reshape(t, blocks), stencil)


def solution(mesh):
    placed = (
        P("phase", None, "gz", "gy"),
        P("phase", "gz", "gy", None),
        P("phase", "gz", "gy", None),
        P(),
    )
    sizes = tuple(mesh.shape[name] for name in ("phase", "gz", "gy"))
    return jax.shard_map(
        functools.partial(body, sizes), mesh=mesh, in_specs=placed,
        out_specs=P("phase", None, "gz", "gy"), check_vma=False,
    )
```
